128 devices in a mesh: row: 32 (over y, x, core), col: 4 (over z).
Axes of the slice: x: 4, y: 4, z: 4, core: 2. Of those that a mesh axis runs over, the one named last changes fastest.
Arguments:
- embeddings: float32 [16384, 256], P(('col', 'row')), may hold values from -6 to 6
- levels: int32 [16384], P('row'), may hold values from 0 to 7
Outputs:
- responsibility: float32 [16384, 16384], P('row', 'col')
- availability: float32 [16384, 16384], P('row', 'col')
The draws below stay inside these ranges and needn't reach their ends.
All inputs are finite; a program needn't handle non-finite values.
Results may differ from the reference program's by a relative error of at most 0.0003.
Values sent between devices are 32-bit elements; how exact they have to be, the bound alone decides.
No kernel may reach another device: no remote copies, remote signals or barrier semaphores. Data moves between devices by JAX's collectives and lax.ppermute only.
A program may use at most 64 MiB of HBM per device.

```python
import jax
import jax.numpy as jnp
from jax import lax

D = 256
ROWS_DEV = 512
ITERS = 2
POINTS = 16384
N_ROW = 32


def with_ends(array, own_key, low, top_value):
    spot = [jax.random.randint(jax.random.fold_in(own_key, axis), (), 0, length) for axis, length in enumerate(array.shape)]
    main_axis = array.shape.index(max(array.shape))
    beside = spot[:main_axis] + [(spot[main_axis] + 1) % array.shape[main_axis]] + spot[main_axis + 1:]
    return array.at[tuple(spot)].set(low).at[tuple(beside)].set(top_value)


def block_levels(key, dims, split, smallest, top_value):
    def one(dim, blocks):
        draws = jax.random.uniform(jax.random.fold_in(jax.random.fold_in(key, 6), dim), (blocks,), jnp.float32, smallest / len(split), top_value / len(split))
        return jnp.repeat(jnp.exp(draws), dims[dim] // blocks).reshape((-1,) + (1,) * (len(dims) - dim - 1))

    level = one(*split[0])
    for cut in split[1:]:
        level = level * one(*cut)
    return level


def bell_draw(stream_key, dims, width, limit, split=(), kind=jnp.bfloat16):
    entries = width * jax.random.normal(stream_key, dims, jnp.float32)
    if split:
        entries = entries * block_levels(stream_key, dims, split, -0.22, 0.18)
    return jnp.clip(entries, -limit, limit).astype(kind)


def setup_inputs(seed: int = 0) -> dict:
    splits = jax.random.split(jax.random.key(seed), 3)
    embeddings = bell_draw(splits[0], (POINTS, D), 1.0, 6.0, ((0, 128),), jnp.float32)
    levels = with_ends(jax.random.randint(splits[1], (POINTS,), 0, 8), jax.random.fold_in(splits[1], 1), 0, 7).astype(jnp.int32)
    return {"embeddings": embeddings, "levels": levels}


lowest_value = -1e+30

def normalize(vectors):
    return vectors * lax.rsqrt(lax.optimization_barrier(jnp.sum(vectors * vectors, axis=1, keepdims=True)) + 1e-06)

def top_two(values):
    best_value = lax.optimization_barrier(jnp.max(values, axis=1, keepdims=True))
    tie_count = lax.optimization_barrier(jnp.sum(jnp.where(values == best_value, 1, 0), axis=1, keepdims=True))
    remainder = lax.optimization_barrier(jnp.max(jnp.where(values < best_value, values, lowest_value), axis=1, keepdims=True))
    return (best_value, jnp.where(tie_count > 1, best_value, remainder))

def reference(embeddings, levels):
    unit_points = normalize(embeddings)
    preference = 0.25 * levels.astype(jnp.float32) - 1.0
    block_ids = jnp.arange(N_ROW, dtype=jnp.int32)
    column_ids = jnp.arange(POINTS, dtype=jnp.int32)
    local_ids = jnp.arange(ROWS_DEV, dtype=jnp.int32)

    def mask_of(block):
        return (block * ROWS_DEV + local_ids)[:, None] == column_ids[None, :]

    def similar_block(block):
        start = block * ROWS_DEV
        row_points = lax.dynamic_slice_in_dim(unit_points, start, ROWS_DEV, 0)
        row_pref = lax.dynamic_slice_in_dim(preference, start, ROWS_DEV, 0)
        product = jnp.dot(row_points, unit_points.T, precision=lax.Precision.HIGHEST, preferred_element_type=jnp.float32)
        return jnp.where(mask_of(block), row_pref[:, None], product)
    similar = lax.map(similar_block, block_ids)
    responsibility = jnp.zeros_like(similar)
    availability = jnp.zeros_like(similar)
    for iteration in range(ITERS):

        def resp_block(inputs):
            sim_rows, avail_rows, resp_rows, block = inputs
            combined = avail_rows + sim_rows
            best_value, second_value = top_two(combined)
            fresh = sim_rows - jnp.where(combined >= best_value, second_value, best_value)
            updated = 0.5 * resp_rows + 0.5 * fresh
            diagonal_mask = mask_of(block)
            positive = lax.optimization_barrier(jnp.sum(jnp.where(diagonal_mask, 0.0, jnp.maximum(updated, 0.0)), axis=0))
            diag_part = lax.optimization_barrier(jnp.sum(jnp.where(diagonal_mask, updated, 0.0), axis=0))
            return (updated, positive, diag_part)
        responsibility, positive, diag_part = lax.map(resp_block, (similar, availability, responsibility, block_ids))
        column_positive = lax.optimization_barrier(jnp.sum(positive, axis=0))
        self_resp = lax.optimization_barrier(jnp.sum(diag_part, axis=0))

        def avail_block(inputs):
            avail_rows, resp_rows, block = inputs
            renewed = jnp.where(mask_of(block), column_positive[None, :], jnp.minimum(0.0, self_resp[None, :] + column_positive[None, :] - jnp.maximum(resp_rows, 0.0)))
            return 0.5 * avail_rows + 0.5 * renewed
        availability = lax.map(avail_block, (availability, responsibility, block_ids))
    return (responsibility.reshape(POINTS, POINTS), availability.reshape(POINTS, POINTS))
```

```python
import jax
import jax.numpy as jnp
from jax import lax
from jax.experimental import pallas as pl
from jax.experimental.pallas import tpu as pltpu
from jax.sharding import PartitionSpec as P

N_ROW, N_COL, SIDE = 32, 4, 4
SHARD, ROWS, D, LANES = 128, 512, 256, 128
BLOCKS = 32
TILE = 64
HOLE = -1e30
BOTH = ("row", "col")
F32 = jnp.float32


def row_of(y, x, core):
    return (y * SIDE + x) * 2 + core


def pairs(target):
    out = []
    for r in range(N_ROW):
        for c in range(N_COL):
            y, x, core = r // 8, r // 2 % 4, r % 2
            to_y, to_x, to_core, to_c = target(y, x, core, c)
            out.append((r * N_COL + c, row_of(to_y, to_x, to_core) * N_COL + to_c))
    return out


def plane_shift(k, stage):
    def target(y, x, core, c):
        if (core == 0) == (stage == 1):
            return y, (x + k) % SIDE, core, c
        return (y + k) % SIDE, x, core, c

    return pairs(target)


def col_shift(k):
    return pairs(lambda y, x, core, c: (y, x, core, (c + k) % N_COL))


def core_swap():
    return pairs(lambda y, x, core, c: (y, x, 1 - core, c))


def to_row_block():
    out = []
    for r in range(N_ROW):
        for j in range(N_COL):
            out.append(((4 * (r % 8) + j) * N_COL + r // 8, r * N_COL + j))
    return out


def permute(a, perm):
    return lax.ppermute(a, BOTH, perm)


def place():
    r, c = lax.axis_index("row"), lax.axis_index("col")
    return r, c


def block_of(n, r):
    k, h, m = n // 8, n // 4 % 2, n % 4
    y, x, core = r // 8, r // 2 % 4, r % 2
    own = core if h == 0 else 1 - core
    a = jnp.where(own == 0, (x - m) % 4, (x - k) % 4)
    b = jnp.where(own == 0, (y - k) % 4, (y - m) % 4)
    return b * 8 + a * 2 + own


def has_diagonal(r, c):
    return jnp.where(r // 8 == c, 1.0, 0.0).astype(F32)


def merge(a, b):
    return jnp.maximum(a[0], b[0]), jnp.maximum(jnp.minimum(a[0], b[0]), jnp.maximum(a[1], b[1]))


def insert(top, x):
    return jnp.maximum(top[0], x), jnp.maximum(top[1], jnp.minimum(top[0], x))


def compact(m1_ref, m2_ref):
    best, second = [], []
    for j in range(4):
        p = (m1_ref[j * 128 : (j + 1) * 128, :].T, m2_ref[j * 128 : (j + 1) * 128, :].T)
        size = 128
        while size > 1:
            size //= 2
            p = merge((p[0][:size], p[1][:size]), (p[0][size:], p[1][size:]))
        best.append(p[0])
        second.append(p[1])
    return jnp.concatenate(best, 0), jnp.concatenate(second, 0)


def store_pair(ref, pair):
    ref[0:4, :] = pair[0]
    ref[4:8, :] = pair[1]


def merged(refs):
    top = (refs[0][0:4, :], refs[0][4:8, :])
    for ref in refs[1:]:
        top = merge(top, (ref[0:4, :], ref[4:8, :]))
    return top


def spread(compacted, ref):
    for j in range(4):
        ref[j * 128 : (j + 1) * 128, :] = jnp.broadcast_to(compacted[j : j + 1, :], (128, 128)).T


def preference(levels_ref):
    return 0.25 * levels_ref[...].astype(F32) - 1.0


def first_diagonal(pref, best, second):
    return 0.5 * (pref - jnp.where(pref >= best, second, best))


def write_sums(acc_ref, tt_ref, diag, r, c, mine_ref, other_ref):
    for n in range(BLOCKS):
        tt_ref[pl.ds(block_of(n, r), 1), :] = jnp.sum(acc_ref[n], axis=0, keepdims=True)
    f = has_diagonal(r, c)
    for j in range(4):
        at = pl.ds(4 * (r % 8) + j, 1)
        tt_ref[at, :] = tt_ref[at, :] + f * diag[j : j + 1, :]
    core = r % 2
    mine_ref[...] = tt_ref[pl.ds(pl.multiple_of(core * 16, 16), 16), :]
    other_ref[...] = tt_ref[pl.ds(pl.multiple_of((1 - core) * 16, 16), 16), :]


def join_sums(mine_ref, other_ref, tt_ref, r):
    core = r % 2
    tt_ref[pl.ds(pl.multiple_of(core * 16, 16), 16), :] = mine_ref[...]
    tt_ref[pl.ds(pl.multiple_of((1 - core) * 16, 16), 16), :] = other_ref[...]


def diagonal_sums(tt_ref, r):
    return jnp.concatenate([tt_ref[pl.ds(4 * (r % 8) + j, 1), :] for j in range(4)], 0)


def unit_kernel(x_ref, o_ref):
    x = x_ref[...]
    o_ref[...] = x * lax.rsqrt(jnp.sum(x * x, axis=1, keepdims=True) + 1e-06)


def split(x):
    high = x.astype(jnp.bfloat16)
    return high, (x - high.astype(F32)).astype(jnp.bfloat16)


def product(a, b):
    dims = (((1,), (1,)), ((), ()))
    dot = lambda p, q: lax.dot_general(p, q, dims, preferred_element_type=F32)
    return dot(a[0], b[0]) + (dot(a[0], b[1]) + dot(a[1], b[0]))


def make_product_kernel(k, first, last):
    def kernel(*refs):
        g, own_ref, partner_ref, refs = refs[:4], refs[4], refs[5], refs[6:]
        if not first:
            in1, in2, refs = refs[0], refs[1], refs[2:]
        if last:
            levels_ref, refs = refs[0], refs[1:]
        s_ref, refs = refs[0], refs[1:]
        if last:
            bs_ref, high, low, m1_ref, m2_ref = refs
        else:
            m1_ref, m2_ref, high, low = refs
        r, c = place()
        for q in range(4):
            h, l = split(g[q][...])
            at = pl.ds(pl.multiple_of((c - q) % 4 * 128, 128), 128)
            high[at, :] = h
            low[at, :] = l
        f = has_diagonal(r, c)
        eye = lax.broadcasted_iota(jnp.int32, (128, 128), 0) == lax.broadcasted_iota(jnp.int32, (128, 128), 1)
        holes = jnp.where(eye, F32(HOLE), F32(0.0))
        for half, ref in enumerate((own_ref, partner_ref)):
            cols = split(ref[...])
            for j in range(4):
                rows = slice(j * 128, (j + 1) * 128)
                p = product((high[rows, :], low[rows, :]), cols)
                if half == 0:
                    if first:
                        top = (jnp.full((128, 128), 2 * HOLE, F32), jnp.full((128, 128), 2 * HOLE, F32))
                    else:
                        top = (in1[rows, :], in2[rows, :])
                else:
                    top = (m1_ref[rows, :], m2_ref[rows, :])
                for m in range(4):
                    n = half * 4 + m
                    here = f * jnp.where(block_of(8 * k + n, r) == 4 * (r % 8) + j, 1.0, 0.0).astype(F32)
                    block = p[:, m * 128 : (m + 1) * 128] + here * holes
                    s_ref[n, rows, :] = block
                    top = insert(top, block)
                m1_ref[rows, :] = top[0]
                m2_ref[rows, :] = top[1]
        if last:
            pair = compact(m1_ref, m2_ref)
            pref = jnp.where(f > 0.0, preference(levels_ref), 2 * HOLE)
            store_pair(bs_ref, insert(pair, pref))

    return kernel


def first_sums_kernel(*refs):
    pieces, levels_ref, s, refs = refs[:4], refs[4], refs[5:9], refs[9:]
    mine_ref, other_ref, bs_ref, b_ref, s_ref, acc_ref, tt_ref = refs
    r, c = place()
    best, second = merged(pieces)
    store_pair(bs_ref, (best, second))
    spread(best, b_ref)
    spread(second, s_ref)
    acc_ref[...] = jnp.zeros_like(acc_ref)

    def body(t, carry):
        rows = pl.ds(pl.multiple_of(t * TILE, TILE), TILE)
        b = b_ref[rows, :]
        v = 0.5 * (b - s_ref[rows, :])
        for n in range(BLOCKS):
            x = jnp.where(s[n // 8][n % 8, rows, :] >= b, v, 0.0)
            acc_ref[n] += jnp.sum(x.reshape(TILE // 8, 8, LANES), axis=0)
        return carry

    lax.fori_loop(0, ROWS // TILE, body, 0)
    diag = first_diagonal(preference(levels_ref), best, second)
    write_sums(acc_ref, tt_ref, diag, r, c, mine_ref, other_ref)


def second_top_kernel(*refs):
    sum1, sum2, bs_ref, levels_ref, b_ref, s_rep, s, refs = *refs[:6], refs[6:10], refs[10:]
    out_ref, half_ref, tt_ref, m1_ref, m2_ref = refs
    r, c = place()
    join_sums(sum1, sum2, tt_ref, r)
    for n in range(BLOCKS):
        half_ref[n] = jnp.broadcast_to(0.5 * tt_ref[pl.ds(block_of(n, r), 1), :], (8, LANES))

    def body(t, carry):
        rows = pl.ds(pl.multiple_of(t * TILE, TILE), TILE)
        b = b_ref[rows, :]
        v = 0.25 * (b - s_rep[rows, :])
        top = (jnp.full((TILE, LANES), 2 * HOLE, F32), jnp.full((TILE, LANES), 2 * HOLE, F32))
        for n in range(BLOCKS):
            x = s[n // 8][n % 8, rows, :]
            half = jnp.tile(half_ref[n], (TILE // 8, 1))
            top = insert(top, x + jnp.minimum(0.0, half - jnp.where(x >= b, v, 0.0)))
        m1_ref[rows, :] = top[0]
        m2_ref[rows, :] = top[1]
        return carry

    lax.fori_loop(0, ROWS // TILE, body, 0)
    pref = preference(levels_ref)
    diag = first_diagonal(pref, bs_ref[0:4, :], bs_ref[4:8, :])
    entry = 0.5 * (diagonal_sums(tt_ref, r) - diag) + pref
    entry = jnp.where(has_diagonal(r, c) > 0.0, entry, 2 * HOLE)
    store_pair(out_ref, insert(compact(m1_ref, m2_ref), entry))


def eye_of(j_half):
    i = lax.broadcasted_iota(jnp.int32, (TILE, LANES), 0) + j_half * TILE
    return i == lax.broadcasted_iota(jnp.int32, (TILE, LANES), 1)


def second_sums_kernel(*refs):
    pieces, sum1, sum2, bs_ref, levels_ref, half_ref, b_ref, s_rep, s, refs = (
        refs[:4], *refs[4:11], refs[11:15], refs[15:])
    out_hbm, mine_ref, other_ref, out_ref, diag_ref, b2_ref, s2_ref, acc_ref, tt_ref, dd_ref, sem = refs
    r, c = place()
    best2, second2 = merged(pieces)
    spread(best2, b2_ref)
    spread(second2, s2_ref)
    join_sums(sum1, sum2, tt_ref, r)
    pref = preference(levels_ref)
    diag1 = first_diagonal(pref, bs_ref[0:4, :], bs_ref[4:8, :])
    avail1 = 0.5 * (diagonal_sums(tt_ref, r) - diag1)
    entry = avail1 + pref
    diag2 = 0.5 * diag1 + 0.5 * (pref - jnp.where(entry >= best2, second2, best2))
    store_pair(diag_ref, (avail1, diag2))
    for j in range(4):
        dd_ref[j] = jnp.broadcast_to(diag2[j : j + 1, :], (8, LANES))
    acc_ref[...] = jnp.zeros_like(acc_ref)
    inside = r // 8 == c

    def copy(t):
        rows = pl.ds(pl.multiple_of(t * TILE, TILE), TILE)
        return pltpu.make_async_copy(out_ref.at[rows, :], out_hbm.at[rows, :], sem.at[t])

    def body(t, carry):
        rows = pl.ds(pl.multiple_of(t * TILE, TILE), TILE)
        b = b_ref[rows, :]
        s1 = s_rep[rows, :]
        b2 = b2_ref[rows, :]
        s2 = s2_ref[rows, :]
        v = 0.25 * (b - s1)
        bq, sq, bh, sh = 0.25 * b, 0.25 * s1, 0.5 * b2, 0.5 * s2
        for n in range(BLOCKS):
            x = s[n // 8][n % 8, rows, :]
            half = jnp.tile(half_ref[n], (TILE // 8, 1))
            hit = x >= b
            entry = x + jnp.minimum(0.0, half - jnp.where(hit, v, 0.0))
            fresh = 0.75 * x - jnp.where(hit, sq, bq) - jnp.where(entry >= b2, sh, bh)
            out_ref[rows, pl.ds(pl.multiple_of(block_of(n, r) * LANES, LANES), LANES)] = fresh
            acc_ref[n] += jnp.sum(jnp.maximum(fresh, 0.0).reshape(TILE // 8, 8, LANES), axis=0)

        @pl.when(inside)
        def _():
            at = pl.ds(pl.multiple_of((4 * (r % 8) + t // 2) * LANES, LANES), LANES)
            value = jnp.tile(dd_ref[t // 2], (TILE // 8, 1))
            out_ref[rows, at] = jnp.where(eye_of(t % 2), value, out_ref[rows, at])

        copy(t).start()
        return carry

    lax.fori_loop(0, ROWS // TILE, body, 0)
    write_sums(acc_ref, tt_ref, diag2, r, c, mine_ref, other_ref)
    for t in range(ROWS // TILE):
        copy(t).wait()


def last_kernel(*refs):
    sum1, sum2, resp_ref, diag_ref, half_ref, b_ref, s_rep, s, refs = *refs[:7], refs[7:11], refs[11:]
    out_hbm, out_ref, half2_ref, tt_ref, dd_ref, sem = refs
    r, c = place()
    join_sums(sum1, sum2, tt_ref, r)
    for n in range(BLOCKS):
        half2_ref[n] = jnp.broadcast_to(0.5 * tt_ref[pl.ds(block_of(n, r), 1), :], (8, LANES))
    diag = 0.5 * diag_ref[0:4, :] + 0.5 * (diagonal_sums(tt_ref, r) - diag_ref[4:8, :])
    for j in range(4):
        dd_ref[j] = jnp.broadcast_to(diag[j : j + 1, :], (8, LANES))
    inside = r // 8 == c

    def copy(t):
        rows = pl.ds(pl.multiple_of(t * TILE, TILE), TILE)
        return pltpu.make_async_copy(out_ref.at[rows, :], out_hbm.at[rows, :], sem.at[t])

    def body(t, carry):
        rows = pl.ds(pl.multiple_of(t * TILE, TILE), TILE)
        b = b_ref[rows, :]
        v = 0.25 * (b - s_rep[rows, :])
        for n in range(BLOCKS):
            at = pl.ds(pl.multiple_of(block_of(n, r) * LANES, LANES), LANES)
            x = s[n // 8][n % 8, rows, :]
            half = jnp.tile(half_ref[n], (TILE // 8, 1))
            half2 = jnp.tile(half2_ref[n], (TILE // 8, 1))
            before = jnp.minimum(0.0, half - jnp.where(x >= b, v, 0.0))
            renewed = jnp.minimum(0.0, half2 - 0.5 * jnp.maximum(resp_ref[rows, at], 0.0))
            out_ref[rows, at] = 0.5 * before + renewed

        @pl.when(inside)
        def _():
            at = pl.ds(pl.multiple_of((4 * (r % 8) + t // 2) * LANES, LANES), LANES)
            value = jnp.tile(dd_ref[t // 2], (TILE // 8, 1))
            out_ref[rows, at] = jnp.where(eye_of(t % 2), value, out_ref[rows, at])

        copy(t).start()
        return carry

    lax.fori_loop(0, ROWS // TILE, body, 0)
    for t in range(ROWS // TILE):
        copy(t).wait()


def call(kernel, args, outs, scratch=(), name=None):
    vmem = pl.BlockSpec(memory_space=pltpu.VMEM)
    any_space = pl.BlockSpec(memory_space=pl.ANY)
    shapes, specs = [], []
    for shape, where in outs:
        shapes.append(jax.ShapeDtypeStruct(shape, F32))
        specs.append(any_space if where == "hbm" else vmem)
    return pl.pallas_call(
        kernel,
        out_shape=tuple(shapes),
        in_specs=[vmem] * len(args),
        out_specs=tuple(specs),
        scratch_shapes=list(scratch),
        compiler_params=pltpu.CompilerParams(vmem_limit_bytes=56 * 2**20),
        name=name,
    )(*args)


def exchange(pair):
    return [pair] + [permute(pair, col_shift(k)) for k in (1, 3, 2)]


def total(mine, other):
    half = mine + permute(other, core_swap())
    groups = [[r for r in range(N_ROW) if r % 2 == core] for core in (0, 1)]
    copies = jnp.broadcast_to(half, (16, 16, LANES)).reshape(256, LANES)
    copies = lax.all_to_all(copies, "row", 0, 0, tiled=True, axis_index_groups=groups)
    half = copies.reshape(16, 16, LANES).sum(axis=0)
    return half, permute(half, core_swap())


def shards(embeddings, levels):
    levels = levels.reshape(4, LANES)
    unit = call(unit_kernel, [embeddings], [((SHARD, D), "vmem")], name="unit")[0]
    mine = permute(unit, to_row_block())
    line = [unit] + [permute(unit, plane_shift(k, 1)) for k in (1, 2, 3)]
    line = jnp.concatenate(line, axis=0)
    rows = [mine] + [permute(mine, col_shift(k)) for k in (1, 2, 3)]
    own = {0: line}
    for k in (1, 3, 2):
        own[k] = permute(line, plane_shift(k, 2))
    similar, top = {}, ()
    running = [((ROWS, LANES), "vmem")] * 2
    pair = ((8, LANES), "vmem")
    s_out = ((8, ROWS, LANES), "vmem")
    big = pltpu.VMEM((ROWS, LANES), F32)
    for k in (0, 1, 3, 2):
        partner = permute(own[k], core_swap())
        first, last = k == 0, k == 2
        args = rows + [own[k], partner, *top] + ([levels] if last else [])
        outs = [s_out] + ([pair] if last else running)
        scratch = [pltpu.VMEM((ROWS, D), jnp.bfloat16)] * 2 + ([big] * 2 if last else [])
        similar[k], *top = call(make_product_kernel(k, first, last), args, outs, scratch, name=f"product{k}")
    pieces = exchange(top[0])
    s = [similar[k] for k in range(4)]
    half = ((16, LANES), "vmem")
    rep = ((ROWS, LANES), "vmem")
    sums = ((BLOCKS, 8, LANES), "vmem")
    acc, tt = pltpu.VMEM((BLOCKS, 8, LANES), F32), pltpu.VMEM((BLOCKS, LANES), F32)
    small = pltpu.VMEM((4, 8, LANES), F32)
    mine, other, bs, b_rep, s_rep = call(
        first_sums_kernel, pieces + [levels, *s], [half, half, pair, rep, rep], [acc, tt], name="first_sums"
    )
    first = total(mine, other)
    bs2, halves = call(
        second_top_kernel, [*first, bs, levels, b_rep, s_rep, *s], [pair, sums], [tt, big, big], name="second_top"
    )
    pieces = exchange(bs2)
    n_copies = ROWS // TILE
    out = ((ROWS, BLOCKS * LANES), "hbm")
    kept = ((ROWS, BLOCKS * LANES), "vmem")
    responsibility, mine, other, resp, diag = call(
        second_sums_kernel,
        pieces + [*first, bs, levels, halves, b_rep, s_rep, *s],
        [out, half, half, kept, pair],
        [big, big, acc, tt, small, pltpu.SemaphoreType.DMA((n_copies,))],
        name="second_sums",
    )
    second = total(mine, other)
    availability = call(
        last_kernel,
        [*second, resp, diag, halves, b_rep, s_rep, *s],
        [out],
        [pltpu.VMEM((ROWS, BLOCKS * LANES), F32), acc, tt, small, pltpu.SemaphoreType.DMA((n_copies,))],
        name="last",
    )[0]
    return responsibility, availability


def solution(mesh):
    placed = (P(("col", "row"), None), P("row"))
    return jax.shard_map(
        shards,
        mesh=mesh,
        in_specs=placed,
        out_specs=(P("row", "col"), P("row", "col")),
        check_vma=False,
    )
```

```python
import jax
import jax.numpy as jnp
from jax import lax
from jax.experimental import pallas as pl
from jax.experimental.pallas import tpu as pltpu
from jax.sharding import PartitionSpec as P


N_ROW, N_COL, SIDE = 32, 4, 4
SHARD, ROWS, D, LANES = 128, 512, 256, 128
BLOCKS = 32
TILE = 64
HOLE = -1e30
BOTH = ("row", "col")
F32 = jnp.float32


def row_of(y, x, core):
    return (y * SIDE + x) * 2 + core


def pairs(target):
    out = []
    for r in range(N_ROW):
        for c in range(N_COL):
            y, x, core = r // 8, r // 2 % 4, r % 2
            to_y, to_x, to_core, to_c = target(y, x, core, c)
            out.append((r * N_COL + c, row_of(to_y, to_x, to_core) * N_COL + to_c))
    return out


def plane_shift(k, stage):
    def target(y, x, core, c):
        if (core == 0) == (stage == 1):
            return y, (x + k) % SIDE, core, c
        return (y + k) % SIDE, x, core, c

    return pairs(target)


def col_shift(k):
    return pairs(lambda y, x, core, c: (y, x, core, (c + k) % N_COL))


def core_swap():
    return pairs(lambda y, x, core, c: (y, x, 1 - core, c))


def to_row_block():
    out = []
    for r in range(N_ROW):
        for j in range(N_COL):
            out.append(((4 * (r % 8) + j) * N_COL + r // 8, r * N_COL + j))
    return out


def permute(a, perm):
    return lax.ppermute(a, BOTH, perm)


def place():
    r, c = lax.axis_index("row"), lax.axis_index("col")
    return r, c


def block_of(n, r):
    k, h, m = n // 8, n // 4 % 2, n % 4
    y, x, core = r // 8, r // 2 % 4, r % 2
    own = core if h == 0 else 1 - core
    a = jnp.where(own == 0, (x - m) % 4, (x - k) % 4)
    b = jnp.where(own == 0, (y - k) % 4, (y - m) % 4)
    return b * 8 + a * 2 + own


def has_diagonal(r, c):
    return jnp.where(r // 8 == c, 1.0, 0.0).astype(F32)


def merge(a, b):
    return jnp.maximum(a[0], b[0]), jnp.maximum(jnp.minimum(a[0], b[0]), jnp.maximum(a[1], b[1]))


def insert(top, x):
    return jnp.maximum(top[0], x), jnp.maximum(top[1], jnp.minimum(top[0], x))


def compact(m1_ref, m2_ref):
    best, second = [], []
    for j in range(4):
        p = (m1_ref[j * 128 : (j + 1) * 128, :].T, m2_ref[j * 128 : (j + 1) * 128, :].T)
        size = 128
        while size > 1:
            size //= 2
            p = merge((p[0][:size], p[1][:size]), (p[0][size:], p[1][size:]))
        best.append(p[0])
        second.append(p[1])
    return jnp.concatenate(best, 0), jnp.concatenate(second, 0)


def store_pair(ref, pair):
    ref[0:4, :] = pair[0]
    ref[4:8, :] = pair[1]


def merged(refs):
    top = (refs[0][0:4, :], refs[0][4:8, :])
    for ref in refs[1:]:
        top = merge(top, (ref[0:4, :], ref[4:8, :]))
    return top


def spread(compacted, ref):
    for j in range(4):
        ref[j * 128 : (j + 1) * 128, :] = jnp.broadcast_to(compacted[j : j + 1, :], (128, 128)).T


def preference(levels_ref):
    return 0.25 * levels_ref[...].astype(F32) - 1.0


def first_diagonal(pref, best, second):
    return 0.5 * (pref - jnp.where(pref >= best, second, best))


def write_sums(acc_ref, tt_ref, diag, r, c, copies_ref):
    for n in range(BLOCKS):
        tt_ref[pl.ds(block_of(n, r), 1), :] = jnp.sum(acc_ref[n], axis=0, keepdims=True)
    f = has_diagonal(r, c)
    for j in range(4):
        at = pl.ds(4 * (r % 8) + j, 1)
        tt_ref[at, :] = tt_ref[at, :] + f * diag[j : j + 1, :]
    sums = tt_ref[...]
    for i in range(N_ROW):
        copies_ref[i * BLOCKS : (i + 1) * BLOCKS, :] = sums


def join_sums(copies_ref, tt_ref):
    parts = [copies_ref[i * BLOCKS : (i + 1) * BLOCKS, :] for i in range(N_ROW)]
    while len(parts) > 1:
        parts = [p + q for p, q in zip(parts[::2], parts[1::2])]
    tt_ref[...] = parts[0]


def diagonal_sums(tt_ref, r):
    return jnp.concatenate([tt_ref[pl.ds(4 * (r % 8) + j, 1), :] for j in range(4)], 0)


def unit_kernel(x_ref, o_ref):
    x = x_ref[...]
    o_ref[...] = x * lax.rsqrt(jnp.sum(x * x, axis=1, keepdims=True) + 1e-06)


def split(x):
    high = x.astype(jnp.bfloat16)
    return high, (x - high.astype(F32)).astype(jnp.bfloat16)


def product(a, b):
    dims = (((1,), (1,)), ((), ()))
    dot = lambda p, q: lax.dot_general(p, q, dims, preferred_element_type=F32)
    return dot(a[0], b[0]) + (dot(a[0], b[1]) + dot(a[1], b[0]))


def make_product_kernel(k, first, last):
    def kernel(*refs):
        g, own_ref, partner_ref, refs = refs[:4], refs[4], refs[5], refs[6:]
        if not first:
            in1, in2, refs = refs[0], refs[1], refs[2:]
        if last:
            levels_ref, refs = refs[0], refs[1:]
        s_ref, refs = refs[0], refs[1:]
        if last:
            bs_ref, high, low, m1_ref, m2_ref = refs
        else:
            m1_ref, m2_ref, high, low = refs
        r, c = place()
        for q in range(4):
            h, l = split(g[q][...])
            at = pl.ds(pl.multiple_of((c - q) % 4 * 128, 128), 128)
            high[at, :] = h
            low[at, :] = l
        f = has_diagonal(r, c)
        eye = lax.broadcasted_iota(jnp.int32, (128, 128), 0) == lax.broadcasted_iota(jnp.int32, (128, 128), 1)
        holes = jnp.where(eye, F32(HOLE), F32(0.0))
        for half, ref in enumerate((own_ref, partner_ref)):
            cols = split(ref[...])
            for j in range(4):
                rows = slice(j * 128, (j + 1) * 128)
                p = product((high[rows, :], low[rows, :]), cols)
                if half == 0:
                    if first:
                        top = (jnp.full((128, 128), 2 * HOLE, F32), jnp.full((128, 128), 2 * HOLE, F32))
                    else:
                        top = (in1[rows, :], in2[rows, :])
                else:
                    top = (m1_ref[rows, :], m2_ref[rows, :])
                for m in range(4):
                    n = half * 4 + m
                    here = f * jnp.where(block_of(8 * k + n, r) == 4 * (r % 8) + j, 1.0, 0.0).astype(F32)
                    block = p[:, m * 128 : (m + 1) * 128] + here * holes
                    s_ref[n, rows, :] = block
                    top = insert(top, block)
                m1_ref[rows, :] = top[0]
                m2_ref[rows, :] = top[1]
        if last:
            pair = compact(m1_ref, m2_ref)
            pref = jnp.where(f > 0.0, preference(levels_ref), 2 * HOLE)
            store_pair(bs_ref, insert(pair, pref))

    return kernel


def first_sums_kernel(*refs):
    pieces, levels_ref, s, refs = refs[:4], refs[4], refs[5:9], refs[9:]
    copies_ref, bs_ref, b_ref, s_ref, acc_ref, tt_ref = refs
    r, c = place()
    best, second = merged(pieces)
    store_pair(bs_ref, (best, second))
    spread(best, b_ref)
    spread(second, s_ref)
    acc_ref[...] = jnp.zeros_like(acc_ref)

    def body(t, carry):
        rows = pl.ds(pl.multiple_of(t * TILE, TILE), TILE)
        b = b_ref[rows, :]
        v = 0.5 * (b - s_ref[rows, :])
        for n in range(BLOCKS):
            x = jnp.where(s[n // 8][n % 8, rows, :] >= b, v, 0.0)
            acc_ref[n] += jnp.sum(x.reshape(TILE // 8, 8, LANES), axis=0)
        return carry

    lax.fori_loop(0, ROWS // TILE, body, 0)
    diag = first_diagonal(preference(levels_ref), best, second)
    write_sums(acc_ref, tt_ref, diag, r, c, copies_ref)


def second_top_kernel(*refs):
    copies_ref, bs_ref, levels_ref, b_ref, s_rep, s, refs = *refs[:5], refs[5:9], refs[9:]
    out_ref, half_ref, tt_ref, m1_ref, m2_ref = refs
    r, c = place()
    join_sums(copies_ref, tt_ref)
    for n in range(BLOCKS):
        half_ref[n] = jnp.broadcast_to(0.5 * tt_ref[pl.ds(block_of(n, r), 1), :], (8, LANES))

    def body(t, carry):
        rows = pl.ds(pl.multiple_of(t * TILE, TILE), TILE)
        b = b_ref[rows, :]
        v = 0.25 * (b - s_rep[rows, :])
        top = (jnp.full((TILE, LANES), 2 * HOLE, F32), jnp.full((TILE, LANES), 2 * HOLE, F32))
        for n in range(BLOCKS):
            x = s[n // 8][n % 8, rows, :]
            half = jnp.tile(half_ref[n], (TILE // 8, 1))
            top = insert(top, x + jnp.minimum(0.0, half - jnp.where(x >= b, v, 0.0)))
        m1_ref[rows, :] = top[0]
        m2_ref[rows, :] = top[1]
        return carry

    lax.fori_loop(0, ROWS // TILE, body, 0)
    pref = preference(levels_ref)
    diag = first_diagonal(pref, bs_ref[0:4, :], bs_ref[4:8, :])
    entry = 0.5 * (diagonal_sums(tt_ref, r) - diag) + pref
    entry = jnp.where(has_diagonal(r, c) > 0.0, entry, 2 * HOLE)
    store_pair(out_ref, insert(compact(m1_ref, m2_ref), entry))


def eye_of(j_half):
    i = lax.broadcasted_iota(jnp.int32, (TILE, LANES), 0) + j_half * TILE
    return i == lax.broadcasted_iota(jnp.int32, (TILE, LANES), 1)


def second_sums_kernel(*refs):
    pieces, sum_ref, bs_ref, levels_ref, half_ref, b_ref, s_rep, s, refs = (
        refs[:4], *refs[4:10], refs[10:14], refs[14:])
    out_hbm, copies_ref, out_ref, diag_ref, b2_ref, s2_ref, acc_ref, tt_ref, dd_ref, sem = refs
    r, c = place()
    best2, second2 = merged(pieces)
    spread(best2, b2_ref)
    spread(second2, s2_ref)
    pref = preference(levels_ref)
    diag1 = first_diagonal(pref, bs_ref[0:4, :], bs_ref[4:8, :])
    avail1 = 0.5 * (diagonal_sums(sum_ref, r) - diag1)
    entry = avail1 + pref
    diag2 = 0.5 * diag1 + 0.5 * (pref - jnp.where(entry >= best2, second2, best2))
    store_pair(diag_ref, (avail1, diag2))
    for j in range(4):
        dd_ref[j] = jnp.broadcast_to(diag2[j : j + 1, :], (8, LANES))
    acc_ref[...] = jnp.zeros_like(acc_ref)
    inside = r // 8 == c

    def copy(t):
        rows = pl.ds(pl.multiple_of(t * TILE, TILE), TILE)
        return pltpu.make_async_copy(out_ref.at[rows, :], out_hbm.at[rows, :], sem.at[t])

    def body(t, carry):
        rows = pl.ds(pl.multiple_of(t * TILE, TILE), TILE)
        b = b_ref[rows, :]
        s1 = s_rep[rows, :]
        b2 = b2_ref[rows, :]
        s2 = s2_ref[rows, :]
        v = 0.25 * (b - s1)
        bq, sq, bh, sh = 0.25 * b, 0.25 * s1, 0.5 * b2, 0.5 * s2
        for n in range(BLOCKS):
            x = s[n // 8][n % 8, rows, :]
            half = jnp.tile(half_ref[n], (TILE // 8, 1))
            hit = x >= b
            entry = x + jnp.minimum(0.0, half - jnp.where(hit, v, 0.0))
            fresh = 0.75 * x - jnp.where(hit, sq, bq) - jnp.where(entry >= b2, sh, bh)
            out_ref[rows, pl.ds(pl.multiple_of(block_of(n, r) * LANES, LANES), LANES)] = fresh
            acc_ref[n] += jnp.sum(jnp.maximum(fresh, 0.0).reshape(TILE // 8, 8, LANES), axis=0)

        @pl.when(inside)
        def _():
            at = pl.ds(pl.multiple_of((4 * (r % 8) + t // 2) * LANES, LANES), LANES)
            value = jnp.tile(dd_ref[t // 2], (TILE // 8, 1))
            out_ref[rows, at] = jnp.where(eye_of(t % 2), value, out_ref[rows, at])

        copy(t).start()
        return carry

    lax.fori_loop(0, ROWS // TILE, body, 0)
    write_sums(acc_ref, tt_ref, diag2, r, c, copies_ref)
    for t in range(ROWS // TILE):
        copy(t).wait()


def last_kernel(*refs):
    copies_ref, resp_ref, diag_ref, half_ref, b_ref, s_rep, s, refs = *refs[:6], refs[6:10], refs[10:]
    out_hbm, out_ref, half2_ref, tt_ref, dd_ref, sem = refs
    r, c = place()
    join_sums(copies_ref, tt_ref)
    for n in range(BLOCKS):
        half2_ref[n] = jnp.broadcast_to(0.5 * tt_ref[pl.ds(block_of(n, r), 1), :], (8, LANES))
    diag = 0.5 * diag_ref[0:4, :] + 0.5 * (diagonal_sums(tt_ref, r) - diag_ref[4:8, :])
    for j in range(4):
        dd_ref[j] = jnp.broadcast_to(diag[j : j + 1, :], (8, LANES))
    inside = r // 8 == c

    def copy(t):
        rows = pl.ds(pl.multiple_of(t * TILE, TILE), TILE)
        return pltpu.make_async_copy(out_ref.at[rows, :], out_hbm.at[rows, :], sem.at[t])

    def body(t, carry):
        rows = pl.ds(pl.multiple_of(t * TILE, TILE), TILE)
        b = b_ref[rows, :]
        v = 0.25 * (b - s_rep[rows, :])
        for n in range(BLOCKS):
            at = pl.ds(pl.multiple_of(block_of(n, r) * LANES, LANES), LANES)
            x = s[n // 8][n % 8, rows, :]
            half = jnp.tile(half_ref[n], (TILE // 8, 1))
            half2 = jnp.tile(half2_ref[n], (TILE // 8, 1))
            before = jnp.minimum(0.0, half - jnp.where(x >= b, v, 0.0))
            renewed = jnp.minimum(0.0, half2 - 0.5 * jnp.maximum(resp_ref[rows, at], 0.0))
            out_ref[rows, at] = 0.5 * before + renewed

        @pl.when(inside)
        def _():
            at = pl.ds(pl.multiple_of((4 * (r % 8) + t // 2) * LANES, LANES), LANES)
            value = jnp.tile(dd_ref[t // 2], (TILE // 8, 1))
            out_ref[rows, at] = jnp.where(eye_of(t % 2), value, out_ref[rows, at])

        copy(t).start()
        return carry

    lax.fori_loop(0, ROWS // TILE, body, 0)
    for t in range(ROWS // TILE):
        copy(t).wait()


def call(kernel, args, outs, scratch=(), megabytes=4):
    vmem = pl.BlockSpec(memory_space=pltpu.VMEM)
    any_space = pl.BlockSpec(memory_space=pl.ANY)
    shapes, specs = [], []
    for shape, where in outs:
        shapes.append(jax.ShapeDtypeStruct(shape, F32) if where == "hbm" else pltpu.VMEM(shape, F32))
        specs.append(any_space if where == "hbm" else vmem)
    args = [pltpu.with_memory_space_constraint(a, pltpu.VMEM) for a in args]
    return pl.pallas_call(
        kernel,
        out_shape=tuple(shapes),
        in_specs=[vmem] * len(args),
        out_specs=tuple(specs),
        scratch_shapes=list(scratch),
        compiler_params=pltpu.CompilerParams(vmem_limit_bytes=megabytes * 2**20),
    )(*args)


def exchange(pair):
    return [pair] + [permute(pair, col_shift(k)) for k in (1, 3, 2)]


def to_all_rows(copies):
    return lax.all_to_all(copies, "row", 0, 0, tiled=True)


def propagate(embeddings, levels):
    levels = levels.reshape(4, LANES)
    unit = call(unit_kernel, [embeddings], [((SHARD, D), "vmem")])[0]
    mine = permute(unit, to_row_block())
    line = [unit] + [permute(unit, plane_shift(k, 1)) for k in (1, 2, 3)]
    line = jnp.concatenate(line, axis=0)
    rows = [mine] + [permute(mine, col_shift(k)) for k in (1, 2, 3)]
    own = {0: line}
    for k in (1, 3, 2):
        own[k] = permute(line, plane_shift(k, 2))
    similar, top = {}, ()
    running = [((ROWS, LANES), "vmem")] * 2
    pair = ((8, LANES), "vmem")
    s_out = ((8, ROWS, LANES), "vmem")
    big = pltpu.VMEM((ROWS, LANES), F32)
    for k in (0, 1, 3, 2):
        partner = permute(own[k], core_swap())
        first, last = k == 0, k == 2
        args = rows + [own[k], partner, *top] + ([levels] if last else [])
        outs = [s_out] + ([pair] if last else running)
        scratch = [pltpu.VMEM((ROWS, D), jnp.bfloat16)] * 2 + ([big] * 2 if last else [])
        similar[k], *top = call(make_product_kernel(k, first, last), args, outs, scratch)
    pieces = exchange(top[0])
    s = [similar[k] for k in range(4)]
    rep = ((ROWS, LANES), "vmem")
    sums = ((BLOCKS, 8, LANES), "vmem")
    flat = ((BLOCKS, LANES), "vmem")
    copies = ((N_ROW * BLOCKS, LANES), "vmem")
    acc, tt = pltpu.VMEM((BLOCKS, 8, LANES), F32), pltpu.VMEM((BLOCKS, LANES), F32)
    small = pltpu.VMEM((4, 8, LANES), F32)
    first, bs, b_rep, s_rep = call(first_sums_kernel, pieces + [levels, *s], [copies, pair, rep, rep], [acc, tt])
    bs2, halves, first = call(
        second_top_kernel, [to_all_rows(first), bs, levels, b_rep, s_rep, *s], [pair, sums, flat], [big, big]
    )
    pieces = exchange(bs2)
    n_copies = ROWS // TILE
    out = ((ROWS, BLOCKS * LANES), "hbm")
    kept = ((ROWS, BLOCKS * LANES), "vmem")
    responsibility, second, resp, diag = call(
        second_sums_kernel,
        pieces + [first, bs, levels, halves, b_rep, s_rep, *s],
        [out, copies, kept, pair],
        [big, big, acc, tt, small, pltpu.SemaphoreType.DMA((n_copies,))],
    )
    availability = call(
        last_kernel,
        [to_all_rows(second), resp, diag, halves, b_rep, s_rep, *s],
        [out],
        [pltpu.VMEM((ROWS, BLOCKS * LANES), F32), acc, tt, small, pltpu.SemaphoreType.DMA((n_copies,))],
        megabytes=12,
    )[0]
    return responsibility, availability


def solution(mesh):
    placed = (P(("col", "row"), None), P("row"))
    return jax.shard_map(
        propagate,
        mesh=mesh,
        in_specs=placed,
        out_specs=(P("row", "col"), P("row", "col")),
        check_vma=False,
    )
```

```python
import jax
import jax.numpy as jnp
from jax import lax
from jax.experimental import pallas as pl
from jax.experimental.pallas import tpu as pltpu
from jax.sharding import PartitionSpec as P


N_ROW, N_COL, SIDE, CHIPS = 32, 4, 4, 16
SHARD, ROWS, D, LANES = 128, 512, 256, 128
BLOCKS = 32
TILE = 64
HOLE = -1e30
BOTH = ("row", "col")
F32 = jnp.float32


def row_of(y, x, core):
    return (y * SIDE + x) * 2 + core


def pairs(target):
    out = []
    for r in range(N_ROW):
        for c in range(N_COL):
            y, x, core = r // 8, r // 2 % 4, r % 2
            to_y, to_x, to_core, to_c = target(y, x, core, c)
            out.append((r * N_COL + c, row_of(to_y, to_x, to_core) * N_COL + to_c))
    return out


def plane_shift(k, stage):
    def target(y, x, core, c):
        if (core == 0) == (stage == 1):
            return y, (x + k) % SIDE, core, c
        return (y + k) % SIDE, x, core, c

    return pairs(target)


def col_shift(k):
    return pairs(lambda y, x, core, c: (y, x, core, (c + k) % N_COL))


def core_swap():
    return pairs(lambda y, x, core, c: (y, x, 1 - core, c))


def to_row_block():
    out = []
    for r in range(N_ROW):
        for j in range(N_COL):
            out.append(((4 * (r % 8) + j) * N_COL + r // 8, r * N_COL + (j + r // 8 + r // 2 % 4) % 4))
    return out


def permute(a, perm):
    return lax.ppermute(a, BOTH, perm)


def place():
    r, c = lax.axis_index("row"), lax.axis_index("col")
    return r, c


def block_of(n, r):
    k, h, m = n // 8, n // 4 % 2, n % 4
    y, x, core = r // 8, r // 2 % 4, r % 2
    own = core if h == 0 else 1 - core
    a = jnp.where(own == 0, (x - m) % 4, (x - k) % 4)
    b = jnp.where(own == 0, (y - k) % 4, (y - m) % 4)
    return b * 8 + a * 2 + own


def has_diagonal(r, c):
    return jnp.where(r // 8 == c, 1.0, 0.0).astype(F32)


def merge(a, b):
    return jnp.maximum(a[0], b[0]), jnp.maximum(jnp.minimum(a[0], b[0]), jnp.maximum(a[1], b[1]))


def insert(top, x):
    return jnp.maximum(top[0], x), jnp.maximum(top[1], jnp.minimum(top[0], x))


def compact(m1_ref, m2_ref):
    best, second = [], []
    for j in range(4):
        p = (m1_ref[j * 128 : (j + 1) * 128, :].T, m2_ref[j * 128 : (j + 1) * 128, :].T)
        size = 128
        while size > 1:
            size //= 2
            p = merge((p[0][:size], p[1][:size]), (p[0][size:], p[1][size:]))
        best.append(p[0])
        second.append(p[1])
    return jnp.concatenate(best, 0), jnp.concatenate(second, 0)


def store_pair(ref, pair):
    ref[0:4, :] = pair[0]
    ref[4:8, :] = pair[1]


def merged(refs):
    top = (refs[0][0:4, :], refs[0][4:8, :])
    for ref in refs[1:]:
        top = merge(top, (ref[0:4, :], ref[4:8, :]))
    return top


def spread(compacted, ref):
    for j in range(4):
        ref[j * 128 : (j + 1) * 128, :] = jnp.broadcast_to(compacted[j : j + 1, :], (128, 128)).T


def first_diagonal(pref, best, second):
    return 0.5 * (pref - jnp.where(pref >= best, second, best))


def write_sums(acc_ref, tt_ref, diag, r, c, out_ref):
    for n in range(BLOCKS):
        tt_ref[pl.ds(block_of(n, r), 1), :] = jnp.sum(acc_ref[n], axis=0, keepdims=True)
    f = has_diagonal(r, c)
    for j in range(4):
        at = pl.ds(4 * (r % 8) + j, 1)
        tt_ref[at, :] = tt_ref[at, :] + f * diag[j : j + 1, :]
    out_ref[...] = tt_ref[...]


def join_sums(copies_ref, tt_ref):
    parts = [copies_ref[i * BLOCKS : (i + 1) * BLOCKS, :] for i in range(CHIPS)]
    while len(parts) > 1:
        parts = [p + q for p, q in zip(parts[::2], parts[1::2])]
    tt_ref[...] = parts[0]


def diagonal_sums(tt_ref, r):
    return jnp.concatenate([tt_ref[pl.ds(4 * (r % 8) + j, 1), :] for j in range(4)], 0)


def unit_kernel(x_ref, levels_ref, o_ref, pref_ref):
    pref_ref[...] = 0.25 * levels_ref[...].astype(F32) - 1.0
    x = x_ref[...]
    o_ref[...] = x * lax.rsqrt(jnp.sum(x * x, axis=1, keepdims=True) + 1e-06)


def split(x):
    high = x.astype(jnp.bfloat16)
    return high, (x - high.astype(F32)).astype(jnp.bfloat16)


def product(a, b):
    return lax.dot_general(a, b, (((1,), (1,)), ((), ())), preferred_element_type=F32)


def make_product_kernel(k, first, last):
    def kernel(*refs):
        refs = list(refs)
        take = lambda count: [refs.pop(0) for _ in range(count)]
        g = take(4) if first else None
        left = None if first else take(1)[0]
        own_ref, partner_ref = take(2)
        in1, in2 = (None, None) if first else take(2)
        pref_ref = take(1)[0] if last else None
        s_ref = take(1)[0]
        if first:
            left = take(1)[0]
        bs_ref = take(1)[0] if last else None
        m1_ref, m2_ref, p_ref = take(3)
        r, c = place()
        if first:
            for q in range(4):
                h, l = split(g[q][...])
                at = pl.ds(pl.multiple_of((c - q - r // 8 - r // 2 % 4) % 4 * 128, 128), 128)
                left[at, 0:D] = h
                left[at, D : 2 * D] = h
                left[at, 2 * D : 3 * D] = l
        f = has_diagonal(r, c)
        eye = lax.broadcasted_iota(jnp.int32, (128, 128), 0) == lax.broadcasted_iota(jnp.int32, (128, 128), 1)
        holes = jnp.where(eye, F32(HOLE), F32(0.0))
        for half, ref in enumerate((own_ref, partner_ref)):
            high, low = split(ref[...])
            right = jnp.concatenate([high, low, high], axis=1)
            p_ref[half] = product(left[...], right)
        for j in range(4):
            rows = slice(j * 128, (j + 1) * 128)
            if first:
                top = (jnp.full((128, 128), 2 * HOLE, F32), jnp.full((128, 128), 2 * HOLE, F32))
            else:
                top = (in1[rows, :], in2[rows, :])
            for n in range(8):
                here = f * jnp.where(block_of(8 * k + n, r) == 4 * (r % 8) + j, 1.0, 0.0).astype(F32)
                block = p_ref[n // 4, rows, n % 4 * 128 : (n % 4 + 1) * 128] + here * holes
                s_ref[n, rows, :] = block
                top = insert(top, block)
            m1_ref[rows, :] = top[0]
            m2_ref[rows, :] = top[1]
        if last:
            pair = compact(m1_ref, m2_ref)
            pref = jnp.where(f > 0.0, pref_ref[...], 2 * HOLE)
            store_pair(bs_ref, insert(pair, pref))

    return kernel


def first_sums_kernel(*refs):
    pieces, pref_ref, s, refs = refs[:4], refs[4], refs[5:9], refs[9:]
    sum_ref, bs_ref, b_ref, s_ref, acc_ref, tt_ref = refs
    r, c = place()
    best, second = merged(pieces)
    store_pair(bs_ref, (best, second))
    spread(best, b_ref)
    spread(second, s_ref)
    acc_ref[...] = jnp.zeros_like(acc_ref)

    def body(t, carry):
        rows = pl.ds(pl.multiple_of(t * TILE, TILE), TILE)
        b = b_ref[rows, :]
        v = 0.5 * (b - s_ref[rows, :])
        for n in range(BLOCKS):
            x = jnp.where(s[n // 8][n % 8, rows, :] >= b, v, 0.0)
            acc_ref[n] += jnp.sum(x.reshape(TILE // 8, 8, LANES), axis=0)
        return carry

    lax.fori_loop(0, ROWS // TILE, body, 0)
    diag = first_diagonal(pref_ref[...], best, second)
    write_sums(acc_ref, tt_ref, diag, r, c, sum_ref)


def copies_kernel(a_ref, b_ref, out_ref):
    both = a_ref[...] + b_ref[...]
    for i in range(CHIPS):
        out_ref[i * BLOCKS : (i + 1) * BLOCKS, :] = both


def second_top_kernel(*refs):
    copies_ref, bs_ref, pref_ref, b_ref, s_rep, s, refs = *refs[:5], refs[5:9], refs[9:]
    out_ref, entry_ref, tt_ref, half_ref, m1_ref, m2_ref = refs
    r, c = place()
    join_sums(copies_ref, tt_ref)
    for n in range(BLOCKS):
        half_ref[n] = jnp.broadcast_to(0.5 * tt_ref[pl.ds(block_of(n, r), 1), :], (8, LANES))

    def body(t, carry):
        rows = pl.ds(pl.multiple_of(t * TILE, TILE), TILE)
        b = b_ref[rows, :]
        v = 0.25 * (b - s_rep[rows, :])
        top = (jnp.full((TILE, LANES), 2 * HOLE, F32), jnp.full((TILE, LANES), 2 * HOLE, F32))
        for n in range(BLOCKS):
            x = s[n // 8][n % 8, rows, :]
            half = jnp.tile(half_ref[n], (TILE // 8, 1))
            entry = x + jnp.minimum(0.0, half - jnp.where(x >= b, v, 0.0))
            entry_ref[n, rows, :] = entry
            top = insert(top, entry)
        m1_ref[rows, :] = top[0]
        m2_ref[rows, :] = top[1]
        return carry

    lax.fori_loop(0, ROWS // TILE, body, 0)
    pref = pref_ref[...]
    diag = first_diagonal(pref, bs_ref[0:4, :], bs_ref[4:8, :])
    entry = 0.5 * (diagonal_sums(tt_ref, r) - diag) + pref
    entry = jnp.where(has_diagonal(r, c) > 0.0, entry, 2 * HOLE)
    store_pair(out_ref, insert(compact(m1_ref, m2_ref), entry))


def eye_of(j_half):
    i = lax.broadcasted_iota(jnp.int32, (TILE, LANES), 0) + j_half * TILE
    return i == lax.broadcasted_iota(jnp.int32, (TILE, LANES), 1)


def second_sums_kernel(*refs):
    pieces, sum_ref, bs_ref, pref_ref, entry_ref, b_ref, s_rep, s, refs = (
        refs[:4], *refs[4:10], refs[10:14], refs[14:])
    out_hbm, sum2_ref, out_ref, diag_ref, b2_ref, s2_ref, acc_ref, tt_ref, dd_ref, sem = refs
    r, c = place()
    best2, second2 = merged(pieces)
    spread(best2, b2_ref)
    spread(second2, s2_ref)
    pref = pref_ref[...]
    diag1 = first_diagonal(pref, bs_ref[0:4, :], bs_ref[4:8, :])
    avail1 = 0.5 * (diagonal_sums(sum_ref, r) - diag1)
    entry = avail1 + pref
    diag2 = 0.5 * diag1 + 0.5 * (pref - jnp.where(entry >= best2, second2, best2))
    store_pair(diag_ref, (avail1, diag2))
    for j in range(4):
        dd_ref[j] = jnp.broadcast_to(diag2[j : j + 1, :], (8, LANES))
    acc_ref[...] = jnp.zeros_like(acc_ref)
    inside = r // 8 == c

    def copy(t):
        rows = pl.ds(pl.multiple_of(t * TILE, TILE), TILE)
        return pltpu.make_async_copy(out_ref.at[rows, :], out_hbm.at[rows, :], sem.at[t])

    def body(t, carry):
        rows = pl.ds(pl.multiple_of(t * TILE, TILE), TILE)
        b, b2 = b_ref[rows, :], b2_ref[rows, :]
        v = 0.25 * (b - s_rep[rows, :])
        v2 = 0.5 * (b2 - s2_ref[rows, :])
        base = 0.25 * b + 0.5 * b2
        for n in range(BLOCKS):
            x = s[n // 8][n % 8, rows, :]
            gain = jnp.where(x >= b, v, 0.0) + jnp.where(entry_ref[n, rows, :] >= b2, v2, 0.0)
            fresh = (0.75 * x - base) + gain
            out_ref[rows, pl.ds(pl.multiple_of(block_of(n, r) * LANES, LANES), LANES)] = fresh
            acc_ref[n] += jnp.sum(jnp.maximum(fresh, 0.0).reshape(TILE // 8, 8, LANES), axis=0)

        @pl.when(inside)
        def _():
            at = pl.ds(pl.multiple_of((4 * (r % 8) + t // 2) * LANES, LANES), LANES)
            value = jnp.tile(dd_ref[t // 2], (TILE // 8, 1))
            out_ref[rows, at] = jnp.where(eye_of(t % 2), value, out_ref[rows, at])

        copy(t).start()
        return carry

    lax.fori_loop(0, ROWS // TILE, body, 0)
    write_sums(acc_ref, tt_ref, diag2, r, c, sum2_ref)
    for t in range(ROWS // TILE):
        copy(t).wait()


def last_kernel(*refs):
    copies_ref, resp_ref, diag_ref, entry_ref, s, refs = *refs[:4], refs[4:8], refs[8:]
    out_hbm, out_ref, total_ref, least_ref, tt_ref, dd_ref, sem = refs
    r, c = place()
    join_sums(copies_ref, tt_ref)
    for n in range(BLOCKS):
        total = jnp.broadcast_to(tt_ref[pl.ds(block_of(n, r), 1), :], (8, LANES))
        total_ref[n] = total
        least_ref[n] = jnp.minimum(0.0, total)
    diag = 0.5 * diag_ref[0:4, :] + 0.5 * (diagonal_sums(tt_ref, r) - diag_ref[4:8, :])
    for j in range(4):
        dd_ref[j] = jnp.broadcast_to(diag[j : j + 1, :], (8, LANES))
    inside = r // 8 == c

    def copy(t):
        rows = pl.ds(pl.multiple_of(t * TILE, TILE), TILE)
        return pltpu.make_async_copy(out_ref.at[rows, :], out_hbm.at[rows, :], sem.at[t])

    def body(t, carry):
        rows = pl.ds(pl.multiple_of(t * TILE, TILE), TILE)
        for n in range(BLOCKS):
            at = pl.ds(pl.multiple_of(block_of(n, r) * LANES, LANES), LANES)
            before = entry_ref[n, rows, :] - s[n // 8][n % 8, rows, :]
            total = jnp.tile(total_ref[n], (TILE // 8, 1))
            least = jnp.tile(least_ref[n], (TILE // 8, 1))
            out_ref[rows, at] = 0.5 * (before + jnp.minimum(least, total - resp_ref[rows, at]))

        @pl.when(inside)
        def _():
            at = pl.ds(pl.multiple_of((4 * (r % 8) + t // 2) * LANES, LANES), LANES)
            value = jnp.tile(dd_ref[t // 2], (TILE // 8, 1))
            out_ref[rows, at] = jnp.where(eye_of(t % 2), value, out_ref[rows, at])

        copy(t).start()
        return carry

    lax.fori_loop(0, ROWS // TILE, body, 0)
    for t in range(ROWS // TILE):
        copy(t).wait()


def call(kernel, args, outs, scratch=(), megabytes=4):
    vmem = pl.BlockSpec(memory_space=pltpu.VMEM)
    any_space = pl.BlockSpec(memory_space=pl.ANY)
    shapes, specs = [], []
    for shape, where in outs:
        dtype = jnp.bfloat16 if where == "bf16" else F32
        shapes.append(jax.ShapeDtypeStruct(shape, F32) if where == "hbm" else pltpu.VMEM(shape, dtype))
        specs.append(any_space if where == "hbm" else vmem)
    args = [pltpu.with_memory_space_constraint(a, pltpu.VMEM) for a in args]
    return pl.pallas_call(
        kernel,
        out_shape=tuple(shapes),
        in_specs=[vmem] * len(args),
        out_specs=tuple(specs),
        scratch_shapes=list(scratch),
        compiler_params=pltpu.CompilerParams(vmem_limit_bytes=megabytes * 2**20),
    )(*args)


def exchange(pair):
    return [pair] + [permute(pair, col_shift(k)) for k in (1, 3, 2)]


def to_all_rows(sums):
    copies = call(copies_kernel, [sums, permute(sums, core_swap())], [((CHIPS * BLOCKS, LANES), "vmem")])[0]
    groups = [[r for r in range(N_ROW) if r % 2 == core] for core in (0, 1)]
    return lax.all_to_all(copies, "row", 0, 0, tiled=True, axis_index_groups=groups)


def propagate(embeddings, levels):
    levels = levels.reshape(4, LANES)
    unit, pref = call(unit_kernel, [embeddings, levels], [((SHARD, D), "vmem"), ((4, LANES), "vmem")])
    mine = permute(unit, to_row_block())
    line = [unit] + [permute(unit, plane_shift(k, 1)) for k in (1, 2, 3)]
    line = jnp.concatenate(line, axis=0)
    rows = [mine] + [permute(mine, col_shift(k)) for k in (1, 2, 3)]
    own = {0: line}
    for k in (1, 3, 2):
        own[k] = permute(line, plane_shift(k, 2))
    similar = {}
    running = [((ROWS, LANES), "vmem")] * 2
    pair = ((8, LANES), "vmem")
    s_out = ((8, ROWS, LANES), "vmem")
    left_out = ((ROWS, 3 * D), "bf16")
    big = pltpu.VMEM((ROWS, LANES), F32)
    parts = pltpu.VMEM((2, ROWS, 4 * LANES), F32)
    for k in (0, 1, 3, 2):
        partner = permute(own[k], core_swap())
        first, last = k == 0, k == 2
        kernel = make_product_kernel(k, first, last)
        if first:
            similar[k], left, *top = call(kernel, rows + [own[k], partner], [s_out, left_out, *running], [parts])
        elif last:
            similar[k], pieces = call(kernel, [left, own[k], partner, *top, pref], [s_out, pair], [big, big, parts])
        else:
            similar[k], *top = call(kernel, [left, own[k], partner, *top], [s_out, *running], [parts])
    pieces = exchange(pieces)
    s = [similar[k] for k in range(4)]
    rep = ((ROWS, LANES), "vmem")
    flat = ((BLOCKS, LANES), "vmem")
    blocks = ((BLOCKS, ROWS, LANES), "vmem")
    acc, tt = pltpu.VMEM((BLOCKS, 8, LANES), F32), pltpu.VMEM((BLOCKS, LANES), F32)
    small = pltpu.VMEM((4, 8, LANES), F32)
    first, bs, b_rep, s_rep = call(first_sums_kernel, pieces + [pref, *s], [flat, pair, rep, rep], [acc, tt])
    bs2, entries, first = call(
        second_top_kernel, [to_all_rows(first), bs, pref, b_rep, s_rep, *s], [pair, blocks, flat], [acc, big, big]
    )
    pieces = exchange(bs2)
    n_copies = ROWS // TILE
    out = ((ROWS, BLOCKS * LANES), "hbm")
    kept = ((ROWS, BLOCKS * LANES), "vmem")
    responsibility, second, resp, diag = call(
        second_sums_kernel,
        pieces + [first, bs, pref, entries, b_rep, s_rep, *s],
        [out, flat, kept, pair],
        [big, big, acc, tt, small, pltpu.SemaphoreType.DMA((n_copies,))],
    )
    availability = call(
        last_kernel,
        [to_all_rows(second), resp, diag, entries, *s],
        [out],
        [pltpu.VMEM((ROWS, BLOCKS * LANES), F32), acc, acc, tt, small, pltpu.SemaphoreType.DMA((n_copies,))],
        megabytes=12,
    )[0]
    return responsibility, availability


def solution(mesh):
    placed = (P(("col", "row"), None), P("row"))
    return jax.shard_map(
        propagate,
        mesh=mesh,
        in_specs=placed,
        out_specs=(P("row", "col"), P("row", "col")),
        check_vma=False,
    )
```

```python
import jax
import jax.numpy as jnp
from jax import lax
from jax.experimental import pallas as pl
from jax.experimental.pallas import tpu as pltpu
from jax.sharding import PartitionSpec as P


N_ROW, N_COL, SIDE, CHIPS = 32, 4, 4, 16
SHARD, ROWS, D, LANES = 128, 512, 256, 128
BLOCKS = 32
TILE = 64
HOLE = -1e30
BOTH = ("row", "col")
F32 = jnp.float32


def row_of(y, x, core):
    return (y * SIDE + x) * 2 + core


def pairs(target):
    out = []
    for r in range(N_ROW):
        for c in range(N_COL):
            y, x, core = r // 8, r // 2 % 4, r % 2
            to_y, to_x, to_core, to_c = target(y, x, core, c)
            out.append((r * N_COL + c, row_of(to_y, to_x, to_core) * N_COL + to_c))
    return out


def plane_shift(k, stage):
    def target(y, x, core, c):
        if (core == 0) == (stage == 1):
            return y, (x + k) % SIDE, core, c
        return (y + k) % SIDE, x, core, c

    return pairs(target)


def col_shift(k):
    return pairs(lambda y, x, core, c: (y, x, core, (c + k) % N_COL))


def core_swap():
    return pairs(lambda y, x, core, c: (y, x, 1 - core, c))


def turn(y, x, core):
    return 2 * (x % 2) + core + y


def col_turn():
    return pairs(lambda y, x, core, c: (y, x, core, (c + turn(y, x, core)) % N_COL))


def to_row_block():
    return pairs(lambda y, x, core, c: ((c - turn(y, x, core)) % N_COL, y, x // 2, c))


def permute(a, perm):
    return lax.ppermute(a, BOTH, perm)


def place():
    r, c = lax.axis_index("row"), lax.axis_index("col")
    return r, c


def block_of(n, r):
    k, h, m = n // 8, n // 4 % 2, n % 4
    y, x, core = r // 8, r // 2 % 4, r % 2
    own = core if h == 0 else 1 - core
    a = jnp.where(own == 0, (x - m) % 4, (x - k) % 4)
    b = jnp.where(own == 0, (y - k) % 4, (y - m) % 4)
    return b * 8 + a * 2 + own


def has_diagonal(r, c):
    return jnp.where(r // 8 == c, 1.0, 0.0).astype(F32)


def merge(a, b):
    return jnp.maximum(a[0], b[0]), jnp.maximum(jnp.minimum(a[0], b[0]), jnp.maximum(a[1], b[1]))


def insert(top, x):
    return jnp.maximum(top[0], x), jnp.maximum(top[1], jnp.minimum(top[0], x))


def compact(m1_ref, m2_ref):
    best, second = [], []
    for j in range(4):
        p = (m1_ref[j * 128 : (j + 1) * 128, :].T, m2_ref[j * 128 : (j + 1) * 128, :].T)
        size = 128
        while size > 1:
            size //= 2
            p = merge((p[0][:size], p[1][:size]), (p[0][size:], p[1][size:]))
        best.append(p[0])
        second.append(p[1])
    return jnp.concatenate(best, 0), jnp.concatenate(second, 0)


def store_pair(ref, pair):
    ref[0:4, :] = pair[0]
    ref[4:8, :] = pair[1]


def merged(refs):
    top = (refs[0][0:4, :], refs[0][4:8, :])
    for ref in refs[1:]:
        top = merge(top, (ref[0:4, :], ref[4:8, :]))
    return top


def spread(compacted, ref):
    for j in range(4):
        ref[j * 128 : (j + 1) * 128, :] = jnp.broadcast_to(compacted[j : j + 1, :], (128, 128)).T


def first_diagonal(pref, best, second):
    return 0.5 * (pref - jnp.where(pref >= best, second, best))


def write_sums(acc_ref, tt_ref, diag, r, c, out_ref):
    for n in range(BLOCKS):
        tt_ref[pl.ds(block_of(n, r), 1), :] = jnp.sum(acc_ref[n], axis=0, keepdims=True)
    f = has_diagonal(r, c)
    for j in range(4):
        at = pl.ds(4 * (r % 8) + j, 1)
        tt_ref[at, :] = tt_ref[at, :] + f * diag[j : j + 1, :]
    out_ref[...] = tt_ref[...]


def join_sums(copies_ref, tt_ref):
    parts = [copies_ref[i * BLOCKS : (i + 1) * BLOCKS, :] for i in range(CHIPS)]
    while len(parts) > 1:
        parts = [p + q for p, q in zip(parts[::2], parts[1::2])]
    tt_ref[...] = parts[0]


def diagonal_sums(tt_ref, r):
    return jnp.concatenate([tt_ref[pl.ds(4 * (r % 8) + j, 1), :] for j in range(4)], 0)


def unit_kernel(x_ref, levels_ref, o_ref, pref_ref):
    pref_ref[...] = 0.25 * levels_ref[...].astype(F32) - 1.0
    x = x_ref[...]
    o_ref[...] = x * lax.rsqrt(jnp.sum(x * x, axis=1, keepdims=True) + 1e-06)


def split(x):
    high = x.astype(jnp.bfloat16)
    return high, (x - high.astype(F32)).astype(jnp.bfloat16)


def product(a, b):
    return lax.dot_general(a, b, (((1,), (1,)), ((), ())), preferred_element_type=F32)


def make_product_kernel(k, first, last):
    def kernel(*refs):
        refs = list(refs)
        take = lambda count: [refs.pop(0) for _ in range(count)]
        g = take(4) if first else None
        left = None if first else take(1)[0]
        own_ref, partner_ref = take(2)
        in1, in2 = (None, None) if first else take(2)
        pref_ref = take(1)[0] if last else None
        s_ref = take(1)[0]
        if first:
            left = take(1)[0]
        bs_ref = take(1)[0] if last else None
        m1_ref, m2_ref, p_ref = take(3)
        r, c = place()
        if first:
            for q in range(4):
                h, l = split(g[q][...])
                at = pl.ds(pl.multiple_of((c - q - r // 8 - r // 2 % 4) % 4 * 128, 128), 128)
                left[at, 0:D] = h
                left[at, D : 2 * D] = h
                left[at, 2 * D : 3 * D] = l
        f = has_diagonal(r, c)
        eye = lax.broadcasted_iota(jnp.int32, (128, 128), 0) == lax.broadcasted_iota(jnp.int32, (128, 128), 1)
        holes = jnp.where(eye, F32(HOLE), F32(0.0))
        for half, ref in enumerate((own_ref, partner_ref)):
            high, low = split(ref[...])
            right = jnp.concatenate([high, low, high], axis=1)
            p_ref[half] = product(left[...], right)
        for j in range(4):
            rows = slice(j * 128, (j + 1) * 128)
            if first:
                top = (jnp.full((128, 128), 2 * HOLE, F32), jnp.full((128, 128), 2 * HOLE, F32))
            else:
                top = (in1[rows, :], in2[rows, :])
            for n in range(8):
                here = f * jnp.where(block_of(8 * k + n, r) == 4 * (r % 8) + j, 1.0, 0.0).astype(F32)
                block = p_ref[n // 4, rows, n % 4 * 128 : (n % 4 + 1) * 128] + here * holes
                s_ref[n, rows, :] = block
                top = insert(top, block)
            m1_ref[rows, :] = top[0]
            m2_ref[rows, :] = top[1]
        if last:
            pair = compact(m1_ref, m2_ref)
            pref = jnp.where(f > 0.0, pref_ref[...], 2 * HOLE)
            store_pair(bs_ref, insert(pair, pref))

    return kernel


def first_sums_kernel(*refs):
    pieces, pref_ref, s, refs = refs[:4], refs[4], refs[5:9], refs[9:]
    sum_ref, bs_ref, b_ref, s_ref, acc_ref, tt_ref = refs
    r, c = place()
    best, second = merged(pieces)
    store_pair(bs_ref, (best, second))
    spread(best, b_ref)
    spread(second, s_ref)
    acc_ref[...] = jnp.zeros_like(acc_ref)

    def body(t, carry):
        rows = pl.ds(pl.multiple_of(t * TILE, TILE), TILE)
        b = b_ref[rows, :]
        v = 0.5 * (b - s_ref[rows, :])
        for n in range(BLOCKS):
            x = jnp.where(s[n // 8][n % 8, rows, :] >= b, v, 0.0)
            acc_ref[n] += jnp.sum(x.reshape(TILE // 8, 8, LANES), axis=0)
        return carry

    lax.fori_loop(0, ROWS // TILE, body, 0)
    diag = first_diagonal(pref_ref[...], best, second)
    write_sums(acc_ref, tt_ref, diag, r, c, sum_ref)


def copies_kernel(a_ref, b_ref, out_ref):
    both = a_ref[...] + b_ref[...]
    for i in range(CHIPS):
        out_ref[i * BLOCKS : (i + 1) * BLOCKS, :] = both


def second_top_kernel(*refs):
    copies_ref, bs_ref, pref_ref, b_ref, s_rep, s, refs = *refs[:5], refs[5:9], refs[9:]
    out_ref, entry_ref, tt_ref, half_ref, m1_ref, m2_ref = refs
    r, c = place()
    join_sums(copies_ref, tt_ref)
    for n in range(BLOCKS):
        half_ref[n] = jnp.broadcast_to(0.5 * tt_ref[pl.ds(block_of(n, r), 1), :], (8, LANES))

    def body(t, carry):
        rows = pl.ds(pl.multiple_of(t * TILE, TILE), TILE)
        b = b_ref[rows, :]
        v = 0.25 * (b - s_rep[rows, :])
        top = (jnp.full((TILE, LANES), 2 * HOLE, F32), jnp.full((TILE, LANES), 2 * HOLE, F32))
        for n in range(BLOCKS):
            x = s[n // 8][n % 8, rows, :]
            half = jnp.tile(half_ref[n], (TILE // 8, 1))
            entry = x + jnp.minimum(0.0, half - jnp.where(x >= b, v, 0.0))
            entry_ref[n, rows, :] = entry
            top = insert(top, entry)
        m1_ref[rows, :] = top[0]
        m2_ref[rows, :] = top[1]
        return carry

    lax.fori_loop(0, ROWS // TILE, body, 0)
    pref = pref_ref[...]
    diag = first_diagonal(pref, bs_ref[0:4, :], bs_ref[4:8, :])
    entry = 0.5 * (diagonal_sums(tt_ref, r) - diag) + pref
    entry = jnp.where(has_diagonal(r, c) > 0.0, entry, 2 * HOLE)
    store_pair(out_ref, insert(compact(m1_ref, m2_ref), entry))


def eye_of(j_half):
    i = lax.broadcasted_iota(jnp.int32, (TILE, LANES), 0) + j_half * TILE
    return i == lax.broadcasted_iota(jnp.int32, (TILE, LANES), 1)


def second_sums_kernel(*refs):
    pieces, sum_ref, bs_ref, pref_ref, entry_ref, b_ref, s_rep, s, refs = (
        refs[:4], *refs[4:10], refs[10:14], refs[14:])
    out_hbm, sum2_ref, out_ref, diag_ref, b2_ref, s2_ref, acc_ref, tt_ref, dd_ref, sem = refs
    r, c = place()
    best2, second2 = merged(pieces)
    spread(best2, b2_ref)
    spread(second2, s2_ref)
    pref = pref_ref[...]
    diag1 = first_diagonal(pref, bs_ref[0:4, :], bs_ref[4:8, :])
    avail1 = 0.5 * (diagonal_sums(sum_ref, r) - diag1)
    entry = avail1 + pref
    diag2 = 0.5 * diag1 + 0.5 * (pref - jnp.where(entry >= best2, second2, best2))
    store_pair(diag_ref, (avail1, diag2))
    for j in range(4):
        dd_ref[j] = jnp.broadcast_to(diag2[j : j + 1, :], (8, LANES))
    acc_ref[...] = jnp.zeros_like(acc_ref)
    inside = r // 8 == c

    def copy(t):
        rows = pl.ds(pl.multiple_of(t * TILE, TILE), TILE)
        return pltpu.make_async_copy(out_ref.at[rows, :], out_hbm.at[rows, :], sem.at[t])

    def body(t, carry):
        rows = pl.ds(pl.multiple_of(t * TILE, TILE), TILE)
        b, b2 = b_ref[rows, :], b2_ref[rows, :]
        v = 0.25 * (b - s_rep[rows, :])
        v2 = 0.5 * (b2 - s2_ref[rows, :])
        base = 0.25 * b + 0.5 * b2
        for n in range(BLOCKS):
            x = s[n // 8][n % 8, rows, :]
            gain = jnp.where(x >= b, v, 0.0) + jnp.where(entry_ref[n, rows, :] >= b2, v2, 0.0)
            fresh = (0.75 * x - base) + gain
            out_ref[rows, pl.ds(pl.multiple_of(block_of(n, r) * LANES, LANES), LANES)] = fresh
            acc_ref[n] += jnp.sum(jnp.maximum(fresh, 0.0).reshape(TILE // 8, 8, LANES), axis=0)

        @pl.when(inside)
        def _():
            at = pl.ds(pl.multiple_of((4 * (r % 8) + t // 2) * LANES, LANES), LANES)
            value = jnp.tile(dd_ref[t // 2], (TILE // 8, 1))
            out_ref[rows, at] = jnp.where(eye_of(t % 2), value, out_ref[rows, at])

        copy(t).start()
        return carry

    lax.fori_loop(0, ROWS // TILE, body, 0)
    write_sums(acc_ref, tt_ref, diag2, r, c, sum2_ref)
    for t in range(ROWS // TILE):
        copy(t).wait()


def last_kernel(*refs):
    copies_ref, resp_ref, diag_ref, entry_ref, s, refs = *refs[:4], refs[4:8], refs[8:]
    out_hbm, out_ref, total_ref, least_ref, tt_ref, dd_ref, sem = refs
    r, c = place()
    join_sums(copies_ref, tt_ref)
    for n in range(BLOCKS):
        total = jnp.broadcast_to(tt_ref[pl.ds(block_of(n, r), 1), :], (8, LANES))
        total_ref[n] = total
        least_ref[n] = jnp.minimum(0.0, total)
    diag = 0.5 * diag_ref[0:4, :] + 0.5 * (diagonal_sums(tt_ref, r) - diag_ref[4:8, :])
    for j in range(4):
        dd_ref[j] = jnp.broadcast_to(diag[j : j + 1, :], (8, LANES))
    inside = r // 8 == c

    def copy(t):
        rows = pl.ds(pl.multiple_of(t * TILE, TILE), TILE)
        return pltpu.make_async_copy(out_ref.at[rows, :], out_hbm.at[rows, :], sem.at[t])

    def body(t, carry):
        rows = pl.ds(pl.multiple_of(t * TILE, TILE), TILE)
        for n in range(BLOCKS):
            at = pl.ds(pl.multiple_of(block_of(n, r) * LANES, LANES), LANES)
            before = entry_ref[n, rows, :] - s[n // 8][n % 8, rows, :]
            total = jnp.tile(total_ref[n], (TILE // 8, 1))
            least = jnp.tile(least_ref[n], (TILE // 8, 1))
            out_ref[rows, at] = 0.5 * (before + jnp.minimum(least, total - resp_ref[rows, at]))

        @pl.when(inside)
        def _():
            at = pl.ds(pl.multiple_of((4 * (r % 8) + t // 2) * LANES, LANES), LANES)
            value = jnp.tile(dd_ref[t // 2], (TILE // 8, 1))
            out_ref[rows, at] = jnp.where(eye_of(t % 2), value, out_ref[rows, at])

        copy(t).start()
        return carry

    lax.fori_loop(0, ROWS // TILE, body, 0)
    for t in range(ROWS // TILE):
        copy(t).wait()


def call(kernel, args, outs, scratch=(), megabytes=4):
    vmem = pl.BlockSpec(memory_space=pltpu.VMEM)
    any_space = pl.BlockSpec(memory_space=pl.ANY)
    shapes, specs = [], []
    for shape, where in outs:
        dtype = jnp.bfloat16 if where == "bf16" else F32
        shapes.append(jax.ShapeDtypeStruct(shape, F32) if where == "hbm" else pltpu.VMEM(shape, dtype))
        specs.append(any_space if where == "hbm" else vmem)
    args = [pltpu.with_memory_space_constraint(a, pltpu.VMEM) for a in args]
    return pl.pallas_call(
        kernel,
        out_shape=tuple(shapes),
        in_specs=[vmem] * len(args),
        out_specs=tuple(specs),
        scratch_shapes=list(scratch),
        compiler_params=pltpu.CompilerParams(vmem_limit_bytes=megabytes * 2**20),
    )(*args)


def exchange(pair):
    return [pair] + [permute(pair, col_shift(k)) for k in (1, 3, 2)]


def to_all_rows(sums):
    copies = call(copies_kernel, [sums, permute(sums, core_swap())], [((CHIPS * BLOCKS, LANES), "vmem")])[0]
    groups = [[r for r in range(N_ROW) if r % 2 == core] for core in (0, 1)]
    return lax.all_to_all(copies, "row", 0, 0, tiled=True, axis_index_groups=groups)


def propagate(embeddings, levels):
    levels = levels.reshape(4, LANES)
    unit, pref = call(unit_kernel, [embeddings, levels], [((SHARD, D), "vmem"), ((4, LANES), "vmem")])
    mine = permute(permute(unit, col_turn()), to_row_block())
    line = [unit] + [permute(unit, plane_shift(k, 1)) for k in (1, 2, 3)]
    line = jnp.concatenate(line, axis=0)
    rows = [mine] + [permute(mine, col_shift(k)) for k in (1, 2, 3)]
    own = {0: line}
    for k in (1, 3, 2):
        own[k] = permute(line, plane_shift(k, 2))
    similar = {}
    running = [((ROWS, LANES), "vmem")] * 2
    pair = ((8, LANES), "vmem")
    s_out = ((8, ROWS, LANES), "vmem")
    left_out = ((ROWS, 3 * D), "bf16")
    big = pltpu.VMEM((ROWS, LANES), F32)
    parts = pltpu.VMEM((2, ROWS, 4 * LANES), F32)
    for k in (0, 1, 3, 2):
        partner = permute(own[k], core_swap())
        first, last = k == 0, k == 2
        kernel = make_product_kernel(k, first, last)
        if first:
            similar[k], left, *top = call(kernel, rows + [own[k], partner], [s_out, left_out, *running], [parts])
        elif last:
            similar[k], pieces = call(kernel, [left, own[k], partner, *top, pref], [s_out, pair], [big, big, parts])
        else:
            similar[k], *top = call(kernel, [left, own[k], partner, *top], [s_out, *running], [parts])
    pieces = exchange(pieces)
    s = [similar[k] for k in range(4)]
    rep = ((ROWS, LANES), "vmem")
    flat = ((BLOCKS, LANES), "vmem")
    blocks = ((BLOCKS, ROWS, LANES), "vmem")
    acc, tt = pltpu.VMEM((BLOCKS, 8, LANES), F32), pltpu.VMEM((BLOCKS, LANES), F32)
    small = pltpu.VMEM((4, 8, LANES), F32)
    first, bs, b_rep, s_rep = call(first_sums_kernel, pieces + [pref, *s], [flat, pair, rep, rep], [acc, tt])
    bs2, entries, first = call(
        second_top_kernel, [to_all_rows(first), bs, pref, b_rep, s_rep, *s], [pair, blocks, flat], [acc, big, big]
    )
    pieces = exchange(bs2)
    n_copies = ROWS // TILE
    out = ((ROWS, BLOCKS * LANES), "hbm")
    kept = ((ROWS, BLOCKS * LANES), "vmem")
    responsibility, second, resp, diag = call(
        second_sums_kernel,
        pieces + [first, bs, pref, entries, b_rep, s_rep, *s],
        [out, flat, kept, pair],
        [big, big, acc, tt, small, pltpu.SemaphoreType.DMA((n_copies,))],
    )
    availability = call(
        last_kernel,
        [to_all_rows(second), resp, diag, entries, *s],
        [out],
        [pltpu.VMEM((ROWS, BLOCKS * LANES), F32), acc, acc, tt, small, pltpu.SemaphoreType.DMA((n_copies,))],
        megabytes=12,
    )[0]
    return responsibility, availability


def solution(mesh):
    placed = (P(("col", "row"), None), P("row"))
    return jax.shard_map(
        propagate,
        mesh=mesh,
        in_specs=placed,
        out_specs=(P("row", "col"), P("row", "col")),
        check_vma=False,
    )
```

```python
import jax
import jax.numpy as jnp
from jax import lax
from jax.experimental import pallas as pl
from jax.experimental.pallas import tpu as pltpu
from jax.sharding import PartitionSpec as P


N_ROW, N_COL, SIDE, CHIPS = 32, 4, 4, 16
SHARD, ROWS, D, LANES = 128, 512, 256, 128
BLOCKS = 32
TILE = 64
HOLE = -1e30
BOTH = ("row", "col")
F32 = jnp.float32


def row_of(y, x, core):
    return (y * SIDE + x) * 2 + core


def pairs(target):
    out = []
    for r in range(N_ROW):
        for c in range(N_COL):
            y, x, core = r // 8, r // 2 % 4, r % 2
            to_y, to_x, to_core, to_c = target(y, x, core, c)
            out.append((r * N_COL + c, row_of(to_y, to_x, to_core) * N_COL + to_c))
    return out


def plane_shift(k, stage):
    def target(y, x, core, c):
        if (core == 0) == (stage == 1):
            return y, (x + k) % SIDE, core, c
        return (y + k) % SIDE, x, core, c

    return pairs(target)


def col_shift(k):
    return pairs(lambda y, x, core, c: (y, x, core, (c + k) % N_COL))


def core_swap():
    return pairs(lambda y, x, core, c: (y, x, 1 - core, c))


def turn(y, x, core):
    return 2 * (x % 2) + core + y


def col_turn():
    return pairs(lambda y, x, core, c: (y, x, core, (c + turn(y, x, core)) % N_COL))


def to_row_block():
    return pairs(lambda y, x, core, c: ((c - turn(y, x, core)) % N_COL, y, x // 2, c))


def permute(a, perm):
    return lax.ppermute(a, BOTH, perm)


def place():
    r, c = lax.axis_index("row"), lax.axis_index("col")
    return r, c


def block_of(n, r):
    k, h, m = n // 8, n // 4 % 2, n % 4
    y, x, core = r // 8, r // 2 % 4, r % 2
    own = core if h == 0 else 1 - core
    a = jnp.where(own == 0, (x - m) % 4, (x - k) % 4)
    b = jnp.where(own == 0, (y - k) % 4, (y - m) % 4)
    return b * 8 + a * 2 + own


def offsets(at_ref, r):
    for n in range(BLOCKS):
        at_ref[n] = block_of(n, r) * LANES


def has_diagonal(r, c):
    return jnp.where(r // 8 == c, 1.0, 0.0).astype(F32)


def merge(a, b):
    return jnp.maximum(a[0], b[0]), jnp.maximum(jnp.minimum(a[0], b[0]), jnp.maximum(a[1], b[1]))


def insert(top, x):
    return jnp.maximum(top[0], x), jnp.maximum(top[1], jnp.minimum(top[0], x))


def compact(m1_ref, m2_ref):
    best, second = [], []
    for j in range(4):
        p = (m1_ref[j * 128 : (j + 1) * 128, :].T, m2_ref[j * 128 : (j + 1) * 128, :].T)
        size = 128
        while size > 1:
            size //= 2
            p = merge((p[0][:size], p[1][:size]), (p[0][size:], p[1][size:]))
        best.append(p[0])
        second.append(p[1])
    return jnp.concatenate(best, 0), jnp.concatenate(second, 0)


def store_pair(ref, pair):
    ref[0:4, :] = pair[0]
    ref[4:8, :] = pair[1]


def merged(refs):
    top = (refs[0][0:4, :], refs[0][4:8, :])
    for ref in refs[1:]:
        top = merge(top, (ref[0:4, :], ref[4:8, :]))
    return top


def spread(compacted, ref):
    for j in range(4):
        ref[j * 128 : (j + 1) * 128, :] = jnp.broadcast_to(compacted[j : j + 1, :], (128, 128)).T


def first_diagonal(pref, best, second):
    return 0.5 * (pref - jnp.where(pref >= best, second, best))


def write_sums(acc_ref, tt_ref, diag, r, c, out_ref):
    for n in range(BLOCKS):
        tt_ref[pl.ds(block_of(n, r), 1), :] = jnp.sum(acc_ref[n], axis=0, keepdims=True)
    f = has_diagonal(r, c)
    for j in range(4):
        at = pl.ds(4 * (r % 8) + j, 1)
        tt_ref[at, :] = tt_ref[at, :] + f * diag[j : j + 1, :]
    out_ref[...] = tt_ref[...]


def join_sums(copies_ref, tt_ref):
    parts = [copies_ref[i * BLOCKS : (i + 1) * BLOCKS, :] for i in range(CHIPS)]
    while len(parts) > 1:
        parts = [p + q for p, q in zip(parts[::2], parts[1::2])]
    tt_ref[...] = parts[0]


def diagonal_sums(tt_ref, r):
    return jnp.concatenate([tt_ref[pl.ds(4 * (r % 8) + j, 1), :] for j in range(4)], 0)


def unit_kernel(x_ref, levels_ref, o_ref, pref_ref):
    pref_ref[...] = 0.25 * levels_ref[...].astype(F32) - 1.0
    x = x_ref[...]
    o_ref[...] = x * lax.rsqrt(jnp.sum(x * x, axis=1, keepdims=True) + 1e-06)


def split(x):
    high = x.astype(jnp.bfloat16)
    return high, (x - high.astype(F32)).astype(jnp.bfloat16)


def product(a, b):
    return lax.dot_general(a, b, (((1,), (1,)), ((), ())), preferred_element_type=F32)


def make_product_kernel(k, first, last):
    def kernel(*refs):
        refs = list(refs)
        take = lambda count: [refs.pop(0) for _ in range(count)]
        g = take(4) if first else None
        left = None if first else take(1)[0]
        own_ref, partner_ref = take(2)
        in1, in2 = (None, None) if first else take(2)
        pref_ref = take(1)[0] if last else None
        s_ref = take(1)[0]
        if first:
            left = take(1)[0]
        bs_ref = take(1)[0] if last else None
        m1_ref, m2_ref, p_ref = take(3)
        r, c = place()
        if first:
            for q in range(4):
                h, l = split(g[q][...])
                at = pl.ds(pl.multiple_of((c - q - r // 8 - r // 2 % 4) % 4 * 128, 128), 128)
                left[at, 0:D] = h
                left[at, D : 2 * D] = h
                left[at, 2 * D : 3 * D] = l
        f = has_diagonal(r, c)
        eye = lax.broadcasted_iota(jnp.int32, (128, 128), 0) == lax.broadcasted_iota(jnp.int32, (128, 128), 1)
        holes = jnp.where(eye, F32(HOLE), F32(0.0))
        for half, ref in enumerate((own_ref, partner_ref)):
            high, low = split(ref[...])
            right = jnp.concatenate([high, low, high], axis=1)
            p_ref[half] = product(left[...], right)
        for j in range(4):
            rows = slice(j * 128, (j + 1) * 128)
            if first:
                top = (jnp.full((128, 128), 2 * HOLE, F32), jnp.full((128, 128), 2 * HOLE, F32))
            else:
                top = (in1[rows, :], in2[rows, :])
            for n in range(8):
                here = f * jnp.where(block_of(8 * k + n, r) == 4 * (r % 8) + j, 1.0, 0.0).astype(F32)
                block = p_ref[n // 4, rows, n % 4 * 128 : (n % 4 + 1) * 128] + here * holes
                s_ref[n, rows, :] = block
                top = insert(top, block)
            m1_ref[rows, :] = top[0]
            m2_ref[rows, :] = top[1]
        if last:
            pair = compact(m1_ref, m2_ref)
            pref = jnp.where(f > 0.0, pref_ref[...], 2 * HOLE)
            store_pair(bs_ref, insert(pair, pref))

    return kernel


def first_sums_kernel(*refs):
    pieces, pref_ref, s, refs = refs[:4], refs[4], refs[5:9], refs[9:]
    sum_ref, bs_ref, b_ref, s_ref, acc_ref, tt_ref = refs
    r, c = place()
    best, second = merged(pieces)
    store_pair(bs_ref, (best, second))
    spread(best, b_ref)
    spread(second, s_ref)
    acc_ref[...] = jnp.zeros_like(acc_ref)

    def body(t, carry):
        rows = pl.ds(pl.multiple_of(t * TILE, TILE), TILE)
        b = b_ref[rows, :]
        v = 0.5 * (b - s_ref[rows, :])
        for n in range(BLOCKS):
            x = jnp.where(s[n // 8][n % 8, rows, :] >= b, v, 0.0)
            acc_ref[n] += jnp.sum(x.reshape(TILE // 8, 8, LANES), axis=0)
        return carry

    lax.fori_loop(0, ROWS // TILE, body, 0)
    diag = first_diagonal(pref_ref[...], best, second)
    write_sums(acc_ref, tt_ref, diag, r, c, sum_ref)


def copies_kernel(a_ref, b_ref, out_ref):
    both = a_ref[...] + b_ref[...]
    for i in range(CHIPS):
        out_ref[i * BLOCKS : (i + 1) * BLOCKS, :] = both


def second_top_kernel(*refs):
    copies_ref, bs_ref, pref_ref, b_ref, s_rep, s, refs = *refs[:5], refs[5:9], refs[9:]
    out_ref, entry_ref, tt_ref, half_ref, m1_ref, m2_ref = refs
    r, c = place()
    join_sums(copies_ref, tt_ref)
    for n in range(BLOCKS):
        half_ref[n] = jnp.broadcast_to(0.5 * tt_ref[pl.ds(block_of(n, r), 1), :], (8, LANES))

    def body(t, carry):
        rows = pl.ds(pl.multiple_of(t * TILE, TILE), TILE)
        b = b_ref[rows, :]
        v = 0.25 * (b - s_rep[rows, :])
        top = (jnp.full((TILE, LANES), 2 * HOLE, F32), jnp.full((TILE, LANES), 2 * HOLE, F32))
        for n in range(BLOCKS):
            x = s[n // 8][n % 8, rows, :]
            half = jnp.tile(half_ref[n], (TILE // 8, 1))
            entry = x + jnp.minimum(0.0, half - jnp.where(x >= b, v, 0.0))
            entry_ref[n, rows, :] = entry
            top = insert(top, entry)
        m1_ref[rows, :] = top[0]
        m2_ref[rows, :] = top[1]
        return carry

    lax.fori_loop(0, ROWS // TILE, body, 0)
    pref = pref_ref[...]
    diag = first_diagonal(pref, bs_ref[0:4, :], bs_ref[4:8, :])
    entry = 0.5 * (diagonal_sums(tt_ref, r) - diag) + pref
    entry = jnp.where(has_diagonal(r, c) > 0.0, entry, 2 * HOLE)
    store_pair(out_ref, insert(compact(m1_ref, m2_ref), entry))


def eye_of(j_half):
    i = lax.broadcasted_iota(jnp.int32, (TILE, LANES), 0) + j_half * TILE
    return i == lax.broadcasted_iota(jnp.int32, (TILE, LANES), 1)


def second_sums_kernel(*refs):
    pieces, sum_ref, bs_ref, pref_ref, entry_ref, b_ref, s_rep, s, refs = (
        refs[:4], *refs[4:10], refs[10:14], refs[14:])
    out_hbm, sum2_ref, out_ref, diag_ref, b2_ref, s2_ref, acc_ref, tt_ref, dd_ref, sem, at_ref = refs
    r, c = place()
    offsets(at_ref, r)
    best2, second2 = merged(pieces)
    spread(best2, b2_ref)
    spread(second2, s2_ref)
    pref = pref_ref[...]
    diag1 = first_diagonal(pref, bs_ref[0:4, :], bs_ref[4:8, :])
    avail1 = 0.5 * (diagonal_sums(sum_ref, r) - diag1)
    entry = avail1 + pref
    diag2 = 0.5 * diag1 + 0.5 * (pref - jnp.where(entry >= best2, second2, best2))
    store_pair(diag_ref, (avail1, diag2))
    for j in range(4):
        dd_ref[j] = jnp.broadcast_to(diag2[j : j + 1, :], (8, LANES))
    acc_ref[...] = jnp.zeros_like(acc_ref)
    inside = r // 8 == c

    def copy(t):
        rows = pl.ds(pl.multiple_of(t * TILE, TILE), TILE)
        return pltpu.make_async_copy(out_ref.at[rows, :], out_hbm.at[rows, :], sem.at[t])

    def body(t, carry):
        rows = pl.ds(pl.multiple_of(t * TILE, TILE), TILE)
        b, b2 = b_ref[rows, :], b2_ref[rows, :]
        v = 0.25 * (b - s_rep[rows, :])
        v2 = 0.5 * (b2 - s2_ref[rows, :])
        base = 0.25 * b + 0.5 * b2
        for n in range(BLOCKS):
            x = s[n // 8][n % 8, rows, :]
            gain = jnp.where(x >= b, v, 0.0) + jnp.where(entry_ref[n, rows, :] >= b2, v2, 0.0)
            fresh = (0.75 * x - base) + gain
            out_ref[rows, pl.ds(pl.multiple_of(at_ref[n], LANES), LANES)] = fresh
            acc_ref[n] += jnp.sum(jnp.maximum(fresh, 0.0).reshape(TILE // 8, 8, LANES), axis=0)

        @pl.when(inside)
        def _():
            at = pl.ds(pl.multiple_of((4 * (r % 8) + t // 2) * LANES, LANES), LANES)
            value = jnp.tile(dd_ref[t // 2], (TILE // 8, 1))
            out_ref[rows, at] = jnp.where(eye_of(t % 2), value, out_ref[rows, at])

        copy(t).start()
        return carry

    lax.fori_loop(0, ROWS // TILE, body, 0)
    write_sums(acc_ref, tt_ref, diag2, r, c, sum2_ref)
    for t in range(ROWS // TILE):
        copy(t).wait()


def last_kernel(*refs):
    copies_ref, resp_ref, diag_ref, entry_ref, s, refs = *refs[:4], refs[4:8], refs[8:]
    out_hbm, out_ref, total_ref, least_ref, tt_ref, dd_ref, sem, at_ref = refs
    r, c = place()
    offsets(at_ref, r)
    join_sums(copies_ref, tt_ref)
    for n in range(BLOCKS):
        total = jnp.broadcast_to(tt_ref[pl.ds(block_of(n, r), 1), :], (8, LANES))
        total_ref[n] = total
        least_ref[n] = jnp.minimum(0.0, total)
    diag = 0.5 * diag_ref[0:4, :] + 0.5 * (diagonal_sums(tt_ref, r) - diag_ref[4:8, :])
    for j in range(4):
        dd_ref[j] = jnp.broadcast_to(diag[j : j + 1, :], (8, LANES))
    inside = r // 8 == c

    def copy(t):
        rows = pl.ds(pl.multiple_of(t * TILE, TILE), TILE)
        return pltpu.make_async_copy(out_ref.at[rows, :], out_hbm.at[rows, :], sem.at[t])

    def body(t, carry):
        rows = pl.ds(pl.multiple_of(t * TILE, TILE), TILE)
        for n in range(BLOCKS):
            at = pl.ds(pl.multiple_of(at_ref[n], LANES), LANES)
            before = entry_ref[n, rows, :] - s[n // 8][n % 8, rows, :]
            total = jnp.tile(total_ref[n], (TILE // 8, 1))
            least = jnp.tile(least_ref[n], (TILE // 8, 1))
            out_ref[rows, at] = 0.5 * (before + jnp.minimum(least, total - resp_ref[rows, at]))

        @pl.when(inside)
        def _():
            at = pl.ds(pl.multiple_of((4 * (r % 8) + t // 2) * LANES, LANES), LANES)
            value = jnp.tile(dd_ref[t // 2], (TILE // 8, 1))
            out_ref[rows, at] = jnp.where(eye_of(t % 2), value, out_ref[rows, at])

        copy(t).start()
        return carry

    lax.fori_loop(0, ROWS // TILE, body, 0)
    for t in range(ROWS // TILE):
        copy(t).wait()


def call(kernel, args, outs, scratch=(), megabytes=4):
    vmem = pl.BlockSpec(memory_space=pltpu.VMEM)
    any_space = pl.BlockSpec(memory_space=pl.ANY)
    shapes, specs = [], []
    for shape, where in outs:
        dtype = jnp.bfloat16 if where == "bf16" else F32
        shapes.append(jax.ShapeDtypeStruct(shape, F32) if where == "hbm" else pltpu.VMEM(shape, dtype))
        specs.append(any_space if where == "hbm" else vmem)
    args = [pltpu.with_memory_space_constraint(a, pltpu.VMEM) for a in args]
    return pl.pallas_call(
        kernel,
        out_shape=tuple(shapes),
        in_specs=[vmem] * len(args),
        out_specs=tuple(specs),
        scratch_shapes=list(scratch),
        compiler_params=pltpu.CompilerParams(vmem_limit_bytes=megabytes * 2**20),
    )(*args)


def exchange(pair):
    return [pair] + [permute(pair, col_shift(k)) for k in (1, 3, 2)]


def to_all_rows(sums):
    copies = call(copies_kernel, [sums, permute(sums, core_swap())], [((CHIPS * BLOCKS, LANES), "vmem")])[0]
    groups = [[r for r in range(N_ROW) if r % 2 == core] for core in (0, 1)]
    return lax.all_to_all(copies, "row", 0, 0, tiled=True, axis_index_groups=groups)


def propagate(embeddings, levels):
    levels = levels.reshape(4, LANES)
    unit, pref = call(unit_kernel, [embeddings, levels], [((SHARD, D), "vmem"), ((4, LANES), "vmem")])
    mine = permute(permute(unit, col_turn()), to_row_block())
    line = [unit] + [permute(unit, plane_shift(k, 1)) for k in (1, 2, 3)]
    line = jnp.concatenate(line, axis=0)
    rows = [mine] + [permute(mine, col_shift(k)) for k in (1, 2, 3)]
    own = {0: line}
    for k in (1, 3, 2):
        own[k] = permute(line, plane_shift(k, 2))
    similar = {}
    running = [((ROWS, LANES), "vmem")] * 2
    pair = ((8, LANES), "vmem")
    s_out = ((8, ROWS, LANES), "vmem")
    left_out = ((ROWS, 3 * D), "bf16")
    big = pltpu.VMEM((ROWS, LANES), F32)
    parts = pltpu.VMEM((2, ROWS, 4 * LANES), F32)
    for k in (0, 1, 3, 2):
        partner = permute(own[k], core_swap())
        first, last = k == 0, k == 2
        kernel = make_product_kernel(k, first, last)
        if first:
            similar[k], left, *top = call(kernel, rows + [own[k], partner], [s_out, left_out, *running], [parts])
        elif last:
            similar[k], pieces = call(kernel, [left, own[k], partner, *top, pref], [s_out, pair], [big, big, parts])
        else:
            similar[k], *top = call(kernel, [left, own[k], partner, *top], [s_out, *running], [parts])
    pieces = exchange(pieces)
    s = [similar[k] for k in range(4)]
    rep = ((ROWS, LANES), "vmem")
    flat = ((BLOCKS, LANES), "vmem")
    blocks = ((BLOCKS, ROWS, LANES), "vmem")
    acc, tt = pltpu.VMEM((BLOCKS, 8, LANES), F32), pltpu.VMEM((BLOCKS, LANES), F32)
    small = pltpu.VMEM((4, 8, LANES), F32)
    first, bs, b_rep, s_rep = call(first_sums_kernel, pieces + [pref, *s], [flat, pair, rep, rep], [acc, tt])
    bs2, entries, first = call(
        second_top_kernel, [to_all_rows(first), bs, pref, b_rep, s_rep, *s], [pair, blocks, flat], [acc, big, big]
    )
    pieces = exchange(bs2)
    n_copies = ROWS // TILE
    table = pltpu.SMEM((BLOCKS,), jnp.int32)
    out = ((ROWS, BLOCKS * LANES), "hbm")
    kept = ((ROWS, BLOCKS * LANES), "vmem")
    responsibility, second, resp, diag = call(
        second_sums_kernel,
        pieces + [first, bs, pref, entries, b_rep, s_rep, *s],
        [out, flat, kept, pair],
        [big, big, acc, tt, small, pltpu.SemaphoreType.DMA((n_copies,)), table],
    )
    availability = call(
        last_kernel,
        [to_all_rows(second), resp, diag, entries, *s],
        [out],
        [pltpu.VMEM((ROWS, BLOCKS * LANES), F32), acc, acc, tt, small, pltpu.SemaphoreType.DMA((n_copies,)), table],
        megabytes=12,
    )[0]
    return responsibility, availability


def solution(mesh):
    placed = (P(("col", "row"), None), P("row"))
    return jax.shard_map(
        propagate,
        mesh=mesh,
        in_specs=placed,
        out_specs=(P("row", "col"), P("row", "col")),
        check_vma=False,
    )
```

```python
import jax
import jax.numpy as jnp
from jax import lax
from jax.experimental import pallas as pl
from jax.experimental.pallas import tpu as pltpu
from jax.sharding import PartitionSpec as P


N_ROW, N_COL, SIDE, CHIPS = 32, 4, 4, 16
SHARD, ROWS, D, LANES = 128, 512, 256, 128
BLOCKS = 32
TILE = 64
EARLY = 6
HOLE = -1e30
BOTH = ("row", "col")
F32 = jnp.float32


def row_of(y, x, core):
    return (y * SIDE + x) * 2 + core


def pairs(target):
    out = []
    for r in range(N_ROW):
        for c in range(N_COL):
            y, x, core = r // 8, r // 2 % 4, r % 2
            to_y, to_x, to_core, to_c = target(y, x, core, c)
            out.append((r * N_COL + c, row_of(to_y, to_x, to_core) * N_COL + to_c))
    return out


def plane_shift(k, stage):
    def target(y, x, core, c):
        if (core == 0) == (stage == 1):
            return y, (x + k) % SIDE, core, c
        return (y + k) % SIDE, x, core, c

    return pairs(target)


def col_shift(k):
    return pairs(lambda y, x, core, c: (y, x, core, (c + k) % N_COL))


def core_swap():
    return pairs(lambda y, x, core, c: (y, x, 1 - core, c))


def turn(y, x, core):
    return 2 * (x % 2) + core + y


def col_turn():
    return pairs(lambda y, x, core, c: (y, x, core, (c + turn(y, x, core)) % N_COL))


def to_row_block():
    return pairs(lambda y, x, core, c: ((c - turn(y, x, core)) % N_COL, y, x // 2, c))


def permute(a, perm):
    return lax.ppermute(a, BOTH, perm)


def place():
    r, c = lax.axis_index("row"), lax.axis_index("col")
    return r, c


def block_of(n, r):
    k, h, m = n // 8, n // 4 % 2, n % 4
    y, x, core = r // 8, r // 2 % 4, r % 2
    own = core if h == 0 else 1 - core
    a = jnp.where(own == 0, (x - m) % 4, (x - k) % 4)
    b = jnp.where(own == 0, (y - k) % 4, (y - m) % 4)
    return b * 8 + a * 2 + own


def offsets(at_ref, r):
    for n in range(BLOCKS):
        at_ref[n] = block_of(n, r) * LANES


def has_diagonal(r, c):
    return jnp.where(r // 8 == c, 1.0, 0.0).astype(F32)


def merge(a, b):
    return jnp.maximum(a[0], b[0]), jnp.maximum(jnp.minimum(a[0], b[0]), jnp.maximum(a[1], b[1]))


def insert(top, x):
    return jnp.maximum(top[0], x), jnp.maximum(top[1], jnp.minimum(top[0], x))


def compact(m1_ref, m2_ref):
    best, second = [], []
    for j in range(4):
        p = (m1_ref[j * 128 : (j + 1) * 128, :].T, m2_ref[j * 128 : (j + 1) * 128, :].T)
        size = 128
        while size > 1:
            size //= 2
            p = merge((p[0][:size], p[1][:size]), (p[0][size:], p[1][size:]))
        best.append(p[0])
        second.append(p[1])
    return jnp.concatenate(best, 0), jnp.concatenate(second, 0)


def store_pair(ref, pair):
    ref[0:4, :] = pair[0]
    ref[4:8, :] = pair[1]


def merged(refs):
    top = (refs[0][0:4, :], refs[0][4:8, :])
    for ref in refs[1:]:
        top = merge(top, (ref[0:4, :], ref[4:8, :]))
    return top


def spread(compacted, ref):
    for j in range(4):
        ref[j * 128 : (j + 1) * 128, :] = jnp.broadcast_to(compacted[j : j + 1, :], (128, 128)).T


def first_diagonal(pref, best, second):
    return 0.5 * (pref - jnp.where(pref >= best, second, best))


def write_sums(acc_ref, tt_ref, diag, r, c, out_ref):
    for n in range(BLOCKS):
        tt_ref[pl.ds(block_of(n, r), 1), :] = jnp.sum(acc_ref[n], axis=0, keepdims=True)
    f = has_diagonal(r, c)
    for j in range(4):
        at = pl.ds(4 * (r % 8) + j, 1)
        tt_ref[at, :] = tt_ref[at, :] + f * diag[j : j + 1, :]
    out_ref[...] = tt_ref[...]


def join_sums(copies_ref, tt_ref):
    parts = [copies_ref[i * BLOCKS : (i + 1) * BLOCKS, :] for i in range(CHIPS)]
    while len(parts) > 1:
        parts = [p + q for p, q in zip(parts[::2], parts[1::2])]
    tt_ref[...] = parts[0]


def diagonal_sums(tt_ref, r):
    return jnp.concatenate([tt_ref[pl.ds(4 * (r % 8) + j, 1), :] for j in range(4)], 0)


def preference_kernel(levels_ref, pref_ref):
    pref_ref[...] = 0.25 * levels_ref[...].astype(F32) - 1.0


def unit_kernel(x_hbm, o_ref, x_ref, sem):
    copy = pltpu.make_async_copy(x_hbm, x_ref, sem)
    copy.start()
    copy.wait()
    x = x_ref[...]
    o_ref[...] = x * lax.rsqrt(jnp.sum(x * x, axis=1, keepdims=True) + 1e-06)


def split(x):
    high = x.astype(jnp.bfloat16)
    return high, (x - high.astype(F32)).astype(jnp.bfloat16)


def product(a, b):
    return lax.dot_general(a, b, (((1,), (1,)), ((), ())), preferred_element_type=F32)


def make_product_kernel(k, first, last):
    def kernel(*refs):
        refs = list(refs)
        take = lambda count: [refs.pop(0) for _ in range(count)]
        g = take(4) if first else None
        left = None if first else take(1)[0]
        own_ref, partner_ref = take(2)
        in1, in2 = (None, None) if first else take(2)
        pref_ref = take(1)[0] if last else None
        s_ref = take(1)[0]
        if first:
            left = take(1)[0]
        bs_ref = take(1)[0] if last else None
        m1_ref, m2_ref, p_ref = take(3)
        r, c = place()
        if first:
            for q in range(4):
                h, l = split(g[q][...])
                at = pl.ds(pl.multiple_of((c - q - r // 8 - r // 2 % 4) % 4 * 128, 128), 128)
                left[at, 0:D] = h
                left[at, D : 2 * D] = h
                left[at, 2 * D : 3 * D] = l
        f = has_diagonal(r, c)
        eye = lax.broadcasted_iota(jnp.int32, (128, 128), 0) == lax.broadcasted_iota(jnp.int32, (128, 128), 1)
        holes = jnp.where(eye, F32(HOLE), F32(0.0))
        for half, ref in enumerate((own_ref, partner_ref)):
            high, low = split(ref[...])
            right = jnp.concatenate([high, low, high], axis=1)
            p_ref[half] = product(left[...], right)
        for j in range(4):
            rows = slice(j * 128, (j + 1) * 128)
            if first:
                top = (jnp.full((128, 128), 2 * HOLE, F32), jnp.full((128, 128), 2 * HOLE, F32))
            else:
                top = (in1[rows, :], in2[rows, :])
            for n in range(8):
                here = f * jnp.where(block_of(8 * k + n, r) == 4 * (r % 8) + j, 1.0, 0.0).astype(F32)
                block = p_ref[n // 4, rows, n % 4 * 128 : (n % 4 + 1) * 128] + here * holes
                s_ref[n, rows, :] = block
                top = insert(top, block)
            m1_ref[rows, :] = top[0]
            m2_ref[rows, :] = top[1]
        if last:
            pair = compact(m1_ref, m2_ref)
            pref = jnp.where(f > 0.0, pref_ref[...], 2 * HOLE)
            store_pair(bs_ref, insert(pair, pref))

    return kernel


def first_sums_kernel(*refs):
    pieces, pref_ref, s, refs = refs[:4], refs[4], refs[5:9], refs[9:]
    sum_ref, bs_ref, b_ref, s_ref, acc_ref, tt_ref = refs
    r, c = place()
    best, second = merged(pieces)
    store_pair(bs_ref, (best, second))
    spread(best, b_ref)
    spread(second, s_ref)
    acc_ref[...] = jnp.zeros_like(acc_ref)

    def body(t, carry):
        rows = pl.ds(pl.multiple_of(t * TILE, TILE), TILE)
        b = b_ref[rows, :]
        v = 0.5 * (b - s_ref[rows, :])
        for n in range(BLOCKS):
            x = jnp.where(s[n // 8][n % 8, rows, :] >= b, v, 0.0)
            acc_ref[n] += jnp.sum(x.reshape(TILE // 8, 8, LANES), axis=0)
        return carry

    lax.fori_loop(0, ROWS // TILE, body, 0)
    diag = first_diagonal(pref_ref[...], best, second)
    write_sums(acc_ref, tt_ref, diag, r, c, sum_ref)


def copies_kernel(a_ref, b_ref, out_ref):
    both = a_ref[...] + b_ref[...]
    for i in range(CHIPS):
        out_ref[i * BLOCKS : (i + 1) * BLOCKS, :] = both


def second_top_kernel(*refs):
    copies_ref, bs_ref, pref_ref, b_ref, s_rep, s, refs = *refs[:5], refs[5:9], refs[9:]
    out_ref, entry_ref, tt_ref, half_ref, m1_ref, m2_ref = refs
    r, c = place()
    join_sums(copies_ref, tt_ref)
    for n in range(BLOCKS):
        half_ref[n] = jnp.broadcast_to(0.5 * tt_ref[pl.ds(block_of(n, r), 1), :], (8, LANES))

    def body(t, carry):
        rows = pl.ds(pl.multiple_of(t * TILE, TILE), TILE)
        b = b_ref[rows, :]
        v = 0.25 * (b - s_rep[rows, :])
        top = (jnp.full((TILE, LANES), 2 * HOLE, F32), jnp.full((TILE, LANES), 2 * HOLE, F32))
        for n in range(BLOCKS):
            x = s[n // 8][n % 8, rows, :]
            half = jnp.tile(half_ref[n], (TILE // 8, 1))
            entry = x + jnp.minimum(0.0, half - jnp.where(x >= b, v, 0.0))
            entry_ref[n, rows, :] = entry
            top = insert(top, entry)
        m1_ref[rows, :] = top[0]
        m2_ref[rows, :] = top[1]
        return carry

    lax.fori_loop(0, ROWS // TILE, body, 0)
    pref = pref_ref[...]
    diag = first_diagonal(pref, bs_ref[0:4, :], bs_ref[4:8, :])
    entry = 0.5 * (diagonal_sums(tt_ref, r) - diag) + pref
    entry = jnp.where(has_diagonal(r, c) > 0.0, entry, 2 * HOLE)
    store_pair(out_ref, insert(compact(m1_ref, m2_ref), entry))


def eye_of(j_half):
    i = lax.broadcasted_iota(jnp.int32, (TILE, LANES), 0) + j_half * TILE
    return i == lax.broadcasted_iota(jnp.int32, (TILE, LANES), 1)


def second_sums_kernel(*refs):
    pieces, sum_ref, bs_ref, pref_ref, entry_ref, b_ref, s_rep, s, refs = (
        refs[:4], *refs[4:10], refs[10:14], refs[14:])
    out_hbm, sum2_ref, out_ref, diag_ref, b2_ref, s2_ref, acc_ref, tt_ref, dd_ref, sem, at_ref = refs
    r, c = place()
    offsets(at_ref, r)
    best2, second2 = merged(pieces)
    spread(best2, b2_ref)
    spread(second2, s2_ref)
    pref = pref_ref[...]
    diag1 = first_diagonal(pref, bs_ref[0:4, :], bs_ref[4:8, :])
    avail1 = 0.5 * (diagonal_sums(sum_ref, r) - diag1)
    entry = avail1 + pref
    diag2 = 0.5 * diag1 + 0.5 * (pref - jnp.where(entry >= best2, second2, best2))
    store_pair(diag_ref, (avail1, diag2))
    for j in range(4):
        dd_ref[j] = jnp.broadcast_to(diag2[j : j + 1, :], (8, LANES))
    acc_ref[...] = jnp.zeros_like(acc_ref)
    inside = r // 8 == c

    def copy(t):
        rows = pl.ds(pl.multiple_of(t * TILE, TILE), TILE)
        return pltpu.make_async_copy(out_ref.at[rows, :], out_hbm.at[rows, :], sem.at[t])

    def body(t, carry):
        rows = pl.ds(pl.multiple_of(t * TILE, TILE), TILE)
        b, b2 = b_ref[rows, :], b2_ref[rows, :]
        v = 0.25 * (b - s_rep[rows, :])
        v2 = 0.5 * (b2 - s2_ref[rows, :])
        base = 0.25 * b + 0.5 * b2
        for n in range(BLOCKS):
            x = s[n // 8][n % 8, rows, :]
            gain = jnp.where(x >= b, v, 0.0) + jnp.where(entry_ref[n, rows, :] >= b2, v2, 0.0)
            fresh = (0.75 * x - base) + gain
            out_ref[rows, pl.ds(pl.multiple_of(at_ref[n], LANES), LANES)] = fresh
            acc_ref[n] += jnp.sum(jnp.maximum(fresh, 0.0).reshape(TILE // 8, 8, LANES), axis=0)

        @pl.when(inside)
        def _():
            at = pl.ds(pl.multiple_of((4 * (r % 8) + t // 2) * LANES, LANES), LANES)
            value = jnp.tile(dd_ref[t // 2], (TILE // 8, 1))
            out_ref[rows, at] = jnp.where(eye_of(t % 2), value, out_ref[rows, at])


        @pl.when(t < EARLY)
        def _():
            copy(t).start()

        return carry

    lax.fori_loop(0, ROWS // TILE, body, 0)
    write_sums(acc_ref, tt_ref, diag2, r, c, sum2_ref)
    for t in range(EARLY):
        copy(t).wait()


def rest_kernel(resp_ref, given_hbm, out_hbm, sem):
    rows = pl.ds(EARLY * TILE, ROWS - EARLY * TILE)
    copy = pltpu.make_async_copy(resp_ref.at[rows, :], out_hbm.at[rows, :], sem)
    copy.start()
    copy.wait()


def last_kernel(*refs):
    copies_ref, resp_ref, diag_ref, entry_ref, s, refs = *refs[:4], refs[4:8], refs[8:]
    out_hbm, out_ref, total_ref, least_ref, tt_ref, dd_ref, sem, at_ref = refs
    r, c = place()
    offsets(at_ref, r)
    join_sums(copies_ref, tt_ref)
    for n in range(BLOCKS):
        total = jnp.broadcast_to(tt_ref[pl.ds(block_of(n, r), 1), :], (8, LANES))
        total_ref[n] = total
        least_ref[n] = jnp.minimum(0.0, total)
    diag = 0.5 * diag_ref[0:4, :] + 0.5 * (diagonal_sums(tt_ref, r) - diag_ref[4:8, :])
    for j in range(4):
        dd_ref[j] = jnp.broadcast_to(diag[j : j + 1, :], (8, LANES))
    inside = r // 8 == c

    def copy(t):
        rows = pl.ds(pl.multiple_of(t * TILE, TILE), TILE)
        return pltpu.make_async_copy(out_ref.at[rows, :], out_hbm.at[rows, :], sem.at[t])

    def body(t, carry):
        rows = pl.ds(pl.multiple_of(t * TILE, TILE), TILE)
        for n in range(BLOCKS):
            at = pl.ds(pl.multiple_of(at_ref[n], LANES), LANES)
            before = entry_ref[n, rows, :] - s[n // 8][n % 8, rows, :]
            total = jnp.tile(total_ref[n], (TILE // 8, 1))
            least = jnp.tile(least_ref[n], (TILE // 8, 1))
            out_ref[rows, at] = 0.5 * (before + jnp.minimum(least, total - resp_ref[rows, at]))

        @pl.when(inside)
        def _():
            at = pl.ds(pl.multiple_of((4 * (r % 8) + t // 2) * LANES, LANES), LANES)
            value = jnp.tile(dd_ref[t // 2], (TILE // 8, 1))
            out_ref[rows, at] = jnp.where(eye_of(t % 2), value, out_ref[rows, at])

        copy(t).start()
        return carry

    lax.fori_loop(0, ROWS // TILE, body, 0)
    for t in range(ROWS // TILE):
        copy(t).wait()


def call(kernel, args, outs, scratch=(), megabytes=4):
    vmem = pl.BlockSpec(memory_space=pltpu.VMEM)
    any_space = pl.BlockSpec(memory_space=pl.ANY)
    shapes, specs = [], []
    for shape, where in outs:
        dtype = jnp.bfloat16 if where == "bf16" else F32
        shapes.append(jax.ShapeDtypeStruct(shape, F32) if where == "hbm" else pltpu.VMEM(shape, dtype))
        specs.append(any_space if where == "hbm" else vmem)
    args = [pltpu.with_memory_space_constraint(a, pltpu.VMEM) for a in args]
    return pl.pallas_call(
        kernel,
        out_shape=tuple(shapes),
        in_specs=[vmem] * len(args),
        out_specs=tuple(specs),
        scratch_shapes=list(scratch),
        compiler_params=pltpu.CompilerParams(vmem_limit_bytes=megabytes * 2**20),
    )(*args)


def exchange(pair):
    return [pair] + [permute(pair, col_shift(k)) for k in (1, 3, 2)]


def to_all_rows(sums):
    copies = call(copies_kernel, [sums, permute(sums, core_swap())], [((CHIPS * BLOCKS, LANES), "vmem")])[0]
    groups = [[r for r in range(N_ROW) if r % 2 == core] for core in (0, 1)]
    return lax.all_to_all(copies, "row", 0, 0, tiled=True, axis_index_groups=groups)


def propagate(embeddings, levels):
    levels = levels.reshape(4, LANES)
    unit = pl.pallas_call(
        unit_kernel,
        out_shape=pltpu.VMEM((SHARD, D), F32),
        in_specs=[pl.BlockSpec(memory_space=pl.ANY)],
        out_specs=pl.BlockSpec(memory_space=pltpu.VMEM),
        scratch_shapes=[pltpu.VMEM((SHARD, D), F32), pltpu.SemaphoreType.DMA(())],
        compiler_params=pltpu.CompilerParams(vmem_limit_bytes=4 * 2**20),
        name="unit",
    )(embeddings)
    pref = call(preference_kernel, [levels], [((4, LANES), "vmem")])[0]
    mine = permute(permute(unit, col_turn()), to_row_block())
    line = [unit] + [permute(unit, plane_shift(k, 1)) for k in (1, 2, 3)]
    line = jnp.concatenate(line, axis=0)
    rows = [mine] + [permute(mine, col_shift(k)) for k in (1, 2, 3)]
    own = {0: line}
    for k in (1, 3, 2):
        own[k] = permute(line, plane_shift(k, 2))
    similar = {}
    running = [((ROWS, LANES), "vmem")] * 2
    pair = ((8, LANES), "vmem")
    s_out = ((8, ROWS, LANES), "vmem")
    left_out = ((ROWS, 3 * D), "bf16")
    big = pltpu.VMEM((ROWS, LANES), F32)
    parts = pltpu.VMEM((2, ROWS, 4 * LANES), F32)
    for k in (0, 1, 3, 2):
        partner = permute(own[k], core_swap())
        first, last = k == 0, k == 2
        kernel = make_product_kernel(k, first, last)
        if first:
            similar[k], left, *top = call(kernel, rows + [own[k], partner], [s_out, left_out, *running], [parts])
        elif last:
            similar[k], pieces = call(kernel, [left, own[k], partner, *top, pref], [s_out, pair], [big, big, parts])
        else:
            similar[k], *top = call(kernel, [left, own[k], partner, *top], [s_out, *running], [parts])
    pieces = exchange(pieces)
    s = [similar[k] for k in range(4)]
    rep = ((ROWS, LANES), "vmem")
    flat = ((BLOCKS, LANES), "vmem")
    blocks = ((BLOCKS, ROWS, LANES), "vmem")
    acc, tt = pltpu.VMEM((BLOCKS, 8, LANES), F32), pltpu.VMEM((BLOCKS, LANES), F32)
    small = pltpu.VMEM((4, 8, LANES), F32)
    first, bs, b_rep, s_rep = call(first_sums_kernel, pieces + [pref, *s], [flat, pair, rep, rep], [acc, tt])
    bs2, entries, first = call(
        second_top_kernel, [to_all_rows(first), bs, pref, b_rep, s_rep, *s], [pair, blocks, flat], [acc, big, big]
    )
    pieces = exchange(bs2)
    n_copies = ROWS // TILE
    table = pltpu.SMEM((BLOCKS,), jnp.int32)
    out = ((ROWS, BLOCKS * LANES), "hbm")
    kept = ((ROWS, BLOCKS * LANES), "vmem")
    responsibility, second, resp, diag = call(
        second_sums_kernel,
        pieces + [first, bs, pref, entries, b_rep, s_rep, *s],
        [out, flat, kept, pair],
        [big, big, acc, tt, small, pltpu.SemaphoreType.DMA((n_copies,)), table],
    )
    responsibility = pl.pallas_call(
        rest_kernel,
        out_shape=jax.ShapeDtypeStruct((ROWS, BLOCKS * LANES), F32),
        in_specs=[pl.BlockSpec(memory_space=pltpu.VMEM), pl.BlockSpec(memory_space=pl.ANY)],
        out_specs=pl.BlockSpec(memory_space=pl.ANY),
        scratch_shapes=[pltpu.SemaphoreType.DMA(())],
        input_output_aliases={1: 0},
        compiler_params=pltpu.CompilerParams(vmem_limit_bytes=4 * 2**20),
        name="rest",
    )(pltpu.with_memory_space_constraint(resp, pltpu.VMEM), responsibility)
    availability = call(
        last_kernel,
        [to_all_rows(second), resp, diag, entries, *s],
        [out],
        [pltpu.VMEM((ROWS, BLOCKS * LANES), F32), acc, acc, tt, small, pltpu.SemaphoreType.DMA((n_copies,)), table],
        megabytes=12,
    )[0]
    return responsibility, availability


def solution(mesh):
    placed = (P(("col", "row"), None), P("row"))
    return jax.shard_map(
        propagate,
        mesh=mesh,
        in_specs=placed,
        out_specs=(P("row", "col"), P("row", "col")),
        check_vma=False,
    )
```
